512 devices in a mesh: ctx: 64 (over y_hi, z, core), head: 8 (over x, y_lo).
Axes of the slice: x: 4, y: 4 (y_hi: 2, y_lo: 2; y = y_hi * 2 + y_lo), z: 16, core: 2. Of those that a mesh axis runs over, the one named last changes fastest.
Arguments:
- query_rows: bfloat16 [16384, 1024], P(('ctx', 'head')), may hold values from -30 to 30
- key_rows: bfloat16 [16384, 1024], P(('ctx', 'head')), may hold values from -7.2 to 7.2
- value_rows: bfloat16 [16384, 1024], P(('ctx', 'head')), may hold values from -6 to 6
- cotangent: bfloat16 [16384, 1024], P(('ctx', 'head')), may hold values from -3 to 3
- key_taps: float32 [3, 1024], P(None, 'head'), may hold values from 0.2 to 1
- value_taps: float32 [3, 1024], P(None, 'head'), may hold values from 0.2 to 1
Outputs:
- attended: bfloat16 [16384, 1024], P(('ctx', 'head'))
- grad_query: bfloat16 [16384, 1024], P(('ctx', 'head'))
- grad_key: bfloat16 [16384, 1024], P(('ctx', 'head'))
- grad_value: bfloat16 [16384, 1024], P(('ctx', 'head'))
- grad_key_taps: float32 [3, 1024], P(None, 'head')
- grad_value_taps: float32 [3, 1024], P(None, 'head')
The draws below stay inside these ranges and needn't reach their ends.
All inputs are finite; a program needn't handle non-finite values.
Results may differ from the reference program's by a relative error of at most 0.012.
Values may be sent and summed in bfloat16 or wider, within the bound.
A program may use at most 128 MiB of HBM per device.

```python
import jax
import jax.numpy as jnp
from jax import lax

D = 1024
HEADS = 16
TOKENS = 16384


def draw_query_rows(key, part):
    noise_key = jax.random.fold_in(key, 11)
    return jnp.clip(1.5 * jax.random.normal(noise_key, (TOKENS, D), jnp.float32), -6.0, 6.0).astype(jnp.bfloat16)


def draw_key_rows(key, part):
    noise_key = jax.random.fold_in(key, 13)
    return jnp.clip(1.8 * jax.random.normal(noise_key, (TOKENS, D), jnp.float32), -7.2, 7.2).astype(jnp.bfloat16)


def levels(key, extent, split, least, high):
    def one(dim, parts):
        heights = jax.random.uniform(jax.random.fold_in(jax.random.fold_in(key, 6), dim), (parts,), jnp.float32, least / len(split), high / len(split))
        return jnp.repeat(jnp.exp(heights), extent[dim] // parts).reshape((-1,) + (1,) * (len(extent) - dim - 1))

    level = one(*split[0])
    for cut in split[1:]:
        level = level * one(*cut)
    return level


def gaussian(own_key, shape, deviation, most, split=(), dtype=jnp.bfloat16):
    values = jax.random.normal(own_key, shape, jnp.float32) * deviation
    if len(split) > 0:
        values = levels(own_key, shape, split, -0.22, 0.18) * values
    return jnp.clip(values, min=-most, max=most).astype(dtype)


def setup_inputs(seed: int = 0) -> dict:
    arg_keys = jax.random.split(jax.random.key(seed), 7)
    query_rows = draw_query_rows(jax.random.fold_in(arg_keys[6], 71), 0)
    key_rows = draw_key_rows(jax.random.fold_in(arg_keys[6], 71), 0)
    value_rows = gaussian(arg_keys[2], (TOKENS, D), 1.0, 6.0, ((0, 512),))
    cotangent = gaussian(arg_keys[3], (TOKENS, D), 0.5, 3.0, ((0, 512),))
    key_taps = jnp.clip(0.2 + 0.8 * jax.random.uniform(arg_keys[4], (3, D), jnp.float32) ** levels(arg_keys[4], (3, D), ((1, 8),), -0.2, 0.2), 0.2, 1.0)
    value_taps = jnp.clip(0.2 + 0.8 * jax.random.uniform(arg_keys[5], (3, D), jnp.float32) ** levels(arg_keys[5], (3, D), ((1, 8),), -0.2, 0.2), 0.2, 1.0)
    return dict(query_rows=query_rows, key_rows=key_rows, value_rows=value_rows, cotangent=cotangent, key_taps=key_taps, value_taps=value_taps)


def compress(row_data, tap_weights, rim_row):
    channels = row_data.shape[1]
    grouped = row_data.astype(jnp.float32).reshape(-1, 4, channels)
    before = jnp.concatenate([rim_row.astype(jnp.float32)[None, :], grouped[:-1, 3]], axis=0)
    packed = (tap_weights[0] * before + tap_weights[1] * grouped[:, 0] + tap_weights[2] * grouped[:, 1]).astype(jnp.bfloat16)
    return packed, grouped, before


def spread_back(comp_grads, tap_weights, incoming, grouped, before):
    channels = comp_grads.shape[1]
    tail_rows = jnp.concatenate([tap_weights[0] * comp_grads[1:], incoming.astype(jnp.float32)[None, :]], axis=0)
    spread = jnp.stack([tap_weights[1] * comp_grads, tap_weights[2] * comp_grads, jnp.zeros_like(comp_grads), tail_rows], axis=1)
    tap_terms = jnp.stack([jnp.sum(comp_grads * before, axis=0), jnp.sum(comp_grads * grouped[:, 0], axis=0), jnp.sum(comp_grads * grouped[:, 1], axis=0)])
    return spread.reshape(-1, channels).astype(jnp.bfloat16), tap_terms


def one_head(operands):
    query_h, key_h, value_h, cot_h = operands
    scaling = query_h.shape[1] ** -0.5
    scores = jnp.dot(query_h, key_h.T, preferred_element_type=jnp.float32) * scaling
    row_max = jnp.max(scores, axis=1, keepdims=True)
    raised = jnp.exp(scores - row_max)
    weights = (raised / jnp.sum(raised, axis=1, keepdims=True)).astype(jnp.bfloat16)
    attended = jnp.dot(weights, value_h, preferred_element_type=jnp.float32).astype(jnp.bfloat16)
    offset = jnp.sum(cot_h.astype(jnp.float32) * attended.astype(jnp.float32), axis=1, keepdims=True)
    dweights = jnp.dot(cot_h, value_h.T, preferred_element_type=jnp.float32)
    dscores = (weights.astype(jnp.float32) * (dweights - offset)).astype(jnp.bfloat16)
    grad_query = (jnp.dot(dscores, key_h, preferred_element_type=jnp.float32) * scaling).astype(jnp.bfloat16)
    grad_key_comp = jnp.dot(dscores.T, query_h, preferred_element_type=jnp.float32) * scaling
    grad_value_comp = jnp.dot(weights.T, cot_h, preferred_element_type=jnp.float32)
    return attended, grad_query, grad_key_comp, grad_value_comp


def split_heads(matrix):
    return matrix.reshape(matrix.shape[0], HEADS, D // HEADS).transpose(1, 0, 2)


def merge_heads(tensor):
    return tensor.transpose(1, 0, 2).reshape(tensor.shape[1], D)


def reference(query_rows, key_rows, value_rows, cotangent, key_taps, value_taps):
    zero_row = jnp.zeros((D,), jnp.float32)
    key_comp, key_groups, key_before = compress(key_rows, key_taps, zero_row)
    value_comp, value_groups, value_before = compress(value_rows, value_taps, zero_row)
    results = lax.map(one_head, (split_heads(query_rows), split_heads(key_comp), split_heads(value_comp), split_heads(cotangent)))
    attended = merge_heads(results[0])
    grad_query = merge_heads(results[1])
    grad_key_comp = merge_heads(results[2])
    grad_value_comp = merge_heads(results[3])
    grad_key, grad_key_taps = spread_back(grad_key_comp, key_taps, zero_row, key_groups, key_before)
    grad_value, grad_value_taps = spread_back(grad_value_comp, value_taps, zero_row, value_groups, value_before)
    return attended, grad_query, grad_key, grad_value, grad_key_taps, grad_value_taps
```

```python
import functools

import jax
import jax.numpy as jnp
from jax import lax
from jax.experimental import pallas as pl
from jax.experimental.pallas import tpu as pltpu
from jax.sharding import PartitionSpec as P

D = 1024
HEADS = 16
MESH = pl.DeviceIdType.MESH
F32 = jnp.float32
BF16 = jnp.bfloat16


def place(nz):
    ctx = lax.axis_index("ctx")
    head = lax.axis_index("head")
    core = ctx % 2
    z = (ctx // 2) % nz
    y = ctx // (2 * nz)
    return ctx, head, y, z, core


def ctx_of(nz, y, z, core):
    return (y * nz + z) * 2 + core


def remote(src, dst, send, recv, ctx, head):
    return pltpu.make_async_remote_copy(
        src_ref=src, dst_ref=dst, send_sem=send, recv_sem=recv,
        device_id={"ctx": ctx, "head": head}, device_id_type=MESH,
    )


def greet(sem, ctx, head):
    pl.semaphore_signal(sem, inc=1, device_id={"ctx": ctx, "head": head}, device_id_type=MESH)


def col(h, width):
    return pl.ds(pl.multiple_of(h * width, width), width)


def gather_kernel(nz, nh, q_in, k_in, v_in, cot_in, kt, vt,
                  q_out, cot_out, kf, vf, kv,
                  k_loc, v_loc, halo,
                  a_send, a_recv, a_self, h_send, h_recv,
                  y_send, y_recv, r_send, r_recv, l_send, l_recv, c_send, c_recv):
    ctx, head, y, z, core = place(nz)
    nctx = 4 * nz
    rows = q_in.shape[0]
    ch = q_out.shape[1]
    zr, zl = (z + 1) % nz, (z + nz - 1) % nz
    right, left = ctx_of(nz, y, zr, core), ctx_of(nz, y, zl, core)
    across = ctx_of(nz, 1 - y, z, core)
    mate = ctx_of(nz, y, z, 1 - core)
    last = nh - 1
    gives = (head == last) & (ctx < nctx - 1)
    takes = ctx >= 1

    barrier = pltpu.get_barrier_semaphore()
    for p in range(1, nh):
        greet(barrier, ctx, (head + p) % nh)
    for other in (right, left, across, mate):
        greet(barrier, other, head)

    @pl.when(takes)
    def _():
        greet(barrier, ctx - 1, last)

    @pl.when(gives)
    def _():
        pl.semaphore_wait(barrier, nh - 1 + 4 + nh)

    @pl.when(jnp.logical_not(gives))
    def _():
        pl.semaphore_wait(barrier, nh - 1 + 4)

    pairs = ((k_in, k_loc), (v_in, v_loc), (q_in, q_out), (cot_in, cot_out))

    def halo_copies():
        out = []
        for a in range(2):
            for t in range(nh):
                out.append(remote(
                    pairs[a][0].at[pl.ds(rows - 16, 16), pl.ds(t * ch, ch)], halo.at[a],
                    h_send.at[a, t], h_recv.at[a], ctx + 1, t))
        return out

    def swaps(a):
        out = []
        for p in range(1, nh):
            t = (head + p) % nh
            out.append(remote(
                pairs[a][0].at[:, col(t, ch)], pairs[a][1].at[col(head, rows), :],
                a_send.at[a, p - 1], a_recv.at[a, p - 1], ctx, t))
        return out

    def own(a):
        return pltpu.make_async_copy(
            pairs[a][0].at[:, col(head, ch)], pairs[a][1].at[col(head, rows), :], a_self.at[a])

    moves = [swaps(a) for a in range(4)]
    for a in range(2):
        own(a).start()
        for m in moves[a]:
            m.start()

    @pl.when(gives)
    def _():
        for m in halo_copies():
            m.start()

    for a in range(2, 4):
        own(a).start()
        for m in moves[a]:
            m.start()

    @pl.when(jnp.logical_not(takes))
    def _():
        kf[0:8, :] = jnp.zeros((8, ch), F32)
        vf[0:8, :] = jnp.zeros((8, ch), F32)

    @pl.when(takes)
    def _():
        for a, f in ((0, kf), (1, vf)):
            pltpu.make_async_copy(halo.at[a], halo.at[a], h_recv.at[a]).wait()
            f[0:8, :] = halo[a].astype(F32)[8:16, :]

    count = nh * rows // 4
    mine = kv.at[core, z]
    for a, f, taps in ((0, kf, kt), (1, vf, vt)):
        own(a).wait()
        for m in moves[a]:
            m.wait_recv()
        f[pl.ds(8, nh * rows), :] = pairs[a][1][...].astype(F32)
        packed = (taps[0:1, :] * f[pl.ds(7, count, stride=4), :]
                  + taps[1:2, :] * f[pl.ds(8, count, stride=4), :]
                  + taps[2:3, :] * f[pl.ds(9, count, stride=4), :])
        kv[core, z, pl.ds(pl.multiple_of(y * count, count), count), a * ch:(a + 1) * ch] = packed.astype(BF16)

    half = mine.at[pl.ds(pl.multiple_of(y * count, count), count), :]
    step_y = remote(half, half, y_send, y_recv, across, head)
    step_y.start()
    step_y.wait_recv()

    def chunk(zz):
        return kv.at[core, zz]

    def to_mate(zz, n):
        return remote(chunk(zz), chunk(zz), c_send.at[n], c_recv.at[n], mate, head)

    def to_right(s):
        zz = (z + nz - s) % nz
        return remote(chunk(zz), chunk(zz), r_send.at[s], r_recv.at[s], right, head)

    def to_left(s):
        zz = (z + s) % nz
        return remote(chunk(zz), chunk(zz), l_send.at[s], l_recv.at[s], left, head)

    nr, nl = nz // 2, nz // 2 - 1
    mates = []
    for s in range(nr):
        to_right(s).start()
        if s < nl:
            to_left(s).start()
        if s == 0:
            mates.append(to_mate(z, 0))
            mates[-1].start()
        to_right(s).wait_recv()
        if s < nl:
            to_left(s).wait_recv()
        mates.append(to_mate((z + nz - s - 1) % nz, 1 + s))
        mates[-1].start()
        if s < nl:
            mates.append(to_mate((z + s + 1) % nz, 1 + nr + s))
            mates[-1].start()
    for a in range(2, 4):
        own(a).wait()
        for m in moves[a]:
            m.wait_recv()
    for m in mates:
        m.wait()
    for s in range(nr):
        to_right(s).wait_send()
    for s in range(nl):
        to_left(s).wait_send()
    step_y.wait_send()
    for a in range(4):
        for m in moves[a]:
            m.wait_send()

    @pl.when(gives)
    def _():
        for m in halo_copies():
            m.wait_send()


def gather(nz, nh, q, k, v, cot, kt, vt):
    rows, width = q.shape
    ch = width // nh
    length = nh * rows
    count = length // 4
    vm = pl.BlockSpec(memory_space=pltpu.VMEM)
    dma = pltpu.SemaphoreType.DMA
    return pl.pallas_call(
        functools.partial(gather_kernel, nz, nh),
        out_shape=(
            jax.ShapeDtypeStruct((length, ch), BF16),
            jax.ShapeDtypeStruct((length, ch), BF16),
            jax.ShapeDtypeStruct((length + 8, ch), F32),
            jax.ShapeDtypeStruct((length + 8, ch), F32),
            jax.ShapeDtypeStruct((2, nz, 2 * count, 2 * ch), BF16),
        ),
        in_specs=[vm] * 6,
        out_specs=(vm,) * 5,
        scratch_shapes=[
            pltpu.VMEM((length, ch), BF16),
            pltpu.VMEM((length, ch), BF16),
            pltpu.VMEM((2, 16, ch), BF16),
            dma((4, nh - 1)), dma((4, nh - 1)), dma((4,)),
            dma((2, nh)), dma((2,)),
            dma(()), dma(()),
            dma((nz // 2,)), dma((nz // 2,)),
            dma((nz // 2,)), dma((nz // 2,)),
            dma((nz,)), dma((nz,)),
        ],
        compiler_params=pltpu.CompilerParams(
            collective_id=0, has_side_effects=True, vmem_limit_bytes=40 << 20),
        name="gather",
    )(q, k, v, cot, kt, vt)


def scatter_kernel(nz, nh, part, att_in, gq_in, kf, vf, kt, vt,
                   att_out, gq_out, gk_out, gv_out, kt_out, vt_out,
                   pin, rbuf, rout, lbuf, lout, ybuf, yout, spread, gk_loc, gv_loc,
                   edge, edge_in, tap1, tap2,
                   a_send, a_recv, a_self, e_send, e_recv,
                   y_send, y_recv, r_send, r_recv, l_send, l_recv, c_send, c_recv,
                   t_send, t_recv, u_send, u_recv):
    ctx, head, y, z, core = place(nz)
    nctx = 4 * nz
    rows = att_out.shape[0]
    ch = att_in.shape[1]
    count = nh * rows // 4
    zr, zl = (z + 1) % nz, (z + nz - 1) % nz
    right, left = ctx_of(nz, y, zr, core), ctx_of(nz, y, zl, core)
    across = ctx_of(nz, 1 - y, z, core)
    mate = ctx_of(nz, y, z, 1 - core)
    corner = ctx_of(nz, 1 - y, z, 1 - core)
    last = nh - 1
    takes = (head == last) & (ctx < nctx - 1)
    gives = ctx >= 1

    barrier = pltpu.get_barrier_semaphore()
    for p in range(1, nh):
        greet(barrier, ctx, (head + p) % nh)
    for p in range(1, nz):
        greet(barrier, ctx_of(nz, y, (z + p) % nz, core), head)
    for other in (across, mate, corner):
        greet(barrier, other, head)

    @pl.when(takes)
    def _():
        for t in range(nh):
            greet(barrier, ctx + 1, t)

    @pl.when(gives)
    def _():
        pl.semaphore_wait(barrier, nh - 1 + nz - 1 + 3 + 1)

    @pl.when(jnp.logical_not(gives))
    def _():
        pl.semaphore_wait(barrier, nh - 1 + nz - 1 + 3)

    nr, nl = nz // 2, nz // 2 - 1

    def to_mate(zz, n):
        return remote(part.at[1 - core, zz], pin.at[zz], c_send.at[n], c_recv.at[n], mate, head)

    order = []
    for s in range(nr):
        order.append((z + nz // 2 + nz - s) % nz)
        if s < nl:
            order.append((z + nz - nl + s) % nz)
    order.append(z)
    mates = [to_mate(zz, n) for n, zz in enumerate(order)]
    for m in mates:
        m.start()

    pairs = ((att_in, att_out), (gq_in, gq_out), (gk_loc, gk_out), (gv_loc, gv_out))

    def swaps(a):
        out = []
        for p in range(1, nh):
            t = (head + p) % nh
            out.append(remote(
                pairs[a][0].at[col(t, rows), :], pairs[a][1].at[:, col(head, ch)],
                a_send.at[a, p - 1], a_recv.at[a, p - 1], ctx, t))
        return out

    def own(a):
        return pltpu.make_async_copy(
            pairs[a][0].at[col(head, rows), :], pairs[a][1].at[:, col(head, ch)], a_self.at[a])

    moves = [swaps(a) for a in range(4)]
    for a in range(2):
        own(a).start()
        for m in moves[a]:
            m.start()

    def local_sum(n):
        mates[n].wait_recv()
        zz = order[n]
        return part[core, zz].astype(F32) + pin[zz].astype(F32)

    def to_right(s):
        return remote(rout.at[s], rbuf.at[s], r_send.at[s], r_recv.at[s], right, head)

    def to_left(s):
        return remote(lout.at[s], lbuf.at[s], l_send.at[s], l_recv.at[s], left, head)

    n = 0
    for s in range(nr):
        total = local_sum(n)
        n += 1
        if s > 0:
            to_right(s - 1).wait_recv()
            total = total + rbuf[s - 1].astype(F32)
        rout[s] = total.astype(BF16)
        to_right(s).start()
        if s < nl:
            total = local_sum(n)
            n += 1
            if s > 0:
                to_left(s - 1).wait_recv()
                total = total + lbuf[s - 1].astype(F32)
            lout[s] = total.astype(BF16)
            to_left(s).start()
    total = local_sum(n)
    to_left(nl - 1).wait_recv()
    total = total + lbuf[nl - 1].astype(F32)
    to_right(nr - 1).wait_recv()
    rout[nr] = (total + rbuf[nr - 1].astype(F32)).astype(BF16)
    ybuf[...] = total + rbuf[nr - 1].astype(F32)
    theirs = rout.at[nr, pl.ds(pl.multiple_of((1 - y) * count, count), count), :]
    step_y = remote(theirs, yout, y_send, y_recv, across, head)
    step_y.start()
    step_y.wait_recv()
    grads = ybuf[pl.ds(pl.multiple_of(y * count, count), count), :] + yout[...].astype(F32)

    tap1[z, 6:8, :] = jnp.zeros((2, ch), F32)
    for a, f, taps, loc in ((0, kf, kt, gk_loc), (1, vf, vt, gv_loc)):
        g = grads[:, a * ch:(a + 1) * ch]
        spread[a, 0:8, :] = jnp.zeros((8, ch), F32)
        spread[a, pl.ds(nh * rows, 8), :] = jnp.zeros((8, ch), F32)
        spread[a, pl.ds(7, count, stride=4), :] = taps[0:1, :] * g
        spread[a, pl.ds(8, count, stride=4), :] = taps[1:2, :] * g
        spread[a, pl.ds(9, count, stride=4), :] = taps[2:3, :] * g
        spread[a, pl.ds(10, count, stride=4), :] = jnp.zeros((count, ch), F32)
        spread[a, pl.ds(nh * rows + 7, 1), :] = jnp.zeros((1, ch), F32)
        loc[...] = spread[a, pl.ds(8, nh * rows), :].astype(BF16)
        edge[a] = jnp.concatenate([jnp.zeros((8, ch), F32), spread[a, 0:8, :]], axis=0).astype(BF16)
        for t in range(3):
            tap1[z, 3 * a + t:3 * a + t + 1, :] = jnp.sum(
                g * f[pl.ds(7 + t, count, stride=4), :], axis=0, keepdims=True)

    def tap_z():
        out = []
        for p in range(1, nz):
            out.append(remote(tap1.at[z], tap1.at[z], t_send.at[p - 1], t_recv.at[p - 1],
                              ctx_of(nz, y, (z + p) % nz, core), head))
        return out

    def tap_yc():
        out = []
        for m, other in enumerate((across, mate, corner)):
            spot = tap2.at[2 * y + core]
            out.append(remote(spot, spot, u_send.at[m], u_recv.at[m], other, head))
        return out

    def edges():
        return [remote(edge.at[a], edge_in.at[a, head], e_send.at[a], e_recv.at[a, head],
                       ctx - 1, last) for a in range(2)]

    for m in tap_z():
        m.start()

    @pl.when(gives)
    def _():
        for m in edges():
            m.start()

    for a in range(2, 4):
        own(a).start()
        for m in moves[a]:
            m.start()

    for m in tap_z():
        m.wait_recv()
    total = tap1[0]
    for i in range(1, nz):
        total = total + tap1[i]
    tap2[2 * y + core] = total
    for m in tap_yc():
        m.start()

    for a in range(4):
        own(a).wait()
        for m in moves[a]:
            m.wait_recv()

    @pl.when(takes)
    def _():
        for a in range(2):
            for t in range(nh):
                pltpu.make_async_copy(edge_in.at[a, t], edge_in.at[a, t], e_recv.at[a, t]).wait()
                spot = (pl.ds(rows - 16, 16), pl.ds(t * ch, ch))
                out = pairs[2 + a][1]
                out[spot] = (out[spot].astype(F32) + edge_in[a, t].astype(F32)).astype(BF16)

    for m in tap_yc():
        m.wait_recv()
    total = (tap2[0] + tap2[1]) + (tap2[2] + tap2[3])
    kt_out[...] = total[0:3, :]
    vt_out[...] = total[3:6, :]

    for m in mates:
        m.wait_send()
    for s in range(nr):
        to_right(s).wait_send()
    for s in range(nl):
        to_left(s).wait_send()
    step_y.wait_send()
    for a in range(4):
        for m in moves[a]:
            m.wait_send()
    for m in tap_z():
        m.wait_send()
    for m in tap_yc():
        m.wait_send()

    @pl.when(gives)
    def _():
        for m in edges():
            m.wait_send()


def scatter(nz, nh, part, att, gq, kf, vf, kt, vt):
    length, ch = att.shape
    rows = length // nh
    count = length // 4
    vm = pl.BlockSpec(memory_space=pltpu.VMEM)
    dma = pltpu.SemaphoreType.DMA
    nr, nl = nz // 2, nz // 2 - 1
    wide = jax.ShapeDtypeStruct((rows, nh * ch), BF16)
    small = jax.ShapeDtypeStruct((3, ch), F32)
    return pl.pallas_call(
        functools.partial(scatter_kernel, nz, nh),
        out_shape=(wide, wide, wide, wide, small, small),
        in_specs=[vm] * 7,
        out_specs=(vm,) * 6,
        scratch_shapes=[
            pltpu.VMEM((nz, 2 * count, 2 * ch), BF16),
            pltpu.VMEM((nr, 2 * count, 2 * ch), BF16),
            pltpu.VMEM((nr + 1, 2 * count, 2 * ch), BF16),
            pltpu.VMEM((nl, 2 * count, 2 * ch), BF16),
            pltpu.VMEM((nl, 2 * count, 2 * ch), BF16),
            pltpu.VMEM((2 * count, 2 * ch), F32),
            pltpu.VMEM((count, 2 * ch), BF16),
            pltpu.VMEM((2, length + 16, ch), F32),
            pltpu.VMEM((length, ch), BF16),
            pltpu.VMEM((length, ch), BF16),
            pltpu.VMEM((2, 16, ch), BF16),
            pltpu.VMEM((2, nh, 16, ch), BF16),
            pltpu.VMEM((nz, 8, ch), F32),
            pltpu.VMEM((4, 8, ch), F32),
            dma((4, nh - 1)), dma((4, nh - 1)), dma((4,)),
            dma((2,)), dma((2, nh)),
            dma(()), dma(()),
            dma((nr,)), dma((nr,)),
            dma((nl,)), dma((nl,)),
            dma((nz,)), dma((nz,)),
            dma((nz - 1,)), dma((nz - 1,)),
            dma((3,)), dma((3,)),
        ],
        compiler_params=pltpu.CompilerParams(
            collective_id=1, has_side_effects=True, vmem_limit_bytes=40 << 20),
        name="scatter",
    )(part, att, gq, kf, vf, kt, vt)


def attention(q, cot, kv):
    length, channels = q.shape
    head_dim = D // HEADS
    heads = channels // head_dim
    scaling = head_dim ** (-0.5)
    flat = kv.reshape(-1, 2 * channels)
    qh = q.reshape(length, heads, head_dim)
    ch = cot.reshape(length, heads, head_dim)
    kh = flat[:, :channels].reshape(-1, heads, head_dim)
    vh = flat[:, channels:].reshape(-1, heads, head_dim)
    scores = jnp.einsum("qhd,khd->hqk", qh, kh, preferred_element_type=F32) * scaling
    raised = jnp.exp(scores - jnp.max(scores, axis=2, keepdims=True))
    weights = (raised / jnp.sum(raised, axis=2, keepdims=True)).astype(BF16)
    att = jnp.einsum("hqk,khd->qhd", weights, vh, preferred_element_type=F32).astype(BF16)
    offset = jnp.sum(ch.astype(F32) * att.astype(F32), axis=2)
    dweights = jnp.einsum("qhd,khd->hqk", ch, vh, preferred_element_type=F32)
    dscores = (weights.astype(F32) * (dweights - offset.T[:, :, None])).astype(BF16)
    gq = (jnp.einsum("hqk,khd->qhd", dscores, kh, preferred_element_type=F32) * scaling).astype(BF16)
    gk = jnp.einsum("hqk,qhd->khd", dscores, qh, preferred_element_type=F32) * scaling
    gv = jnp.einsum("hqk,qhd->khd", weights, ch, preferred_element_type=F32)
    part = jnp.concatenate(
        [gk.reshape(-1, channels), gv.reshape(-1, channels)], axis=1).astype(BF16)
    return att.reshape(length, channels), gq.reshape(length, channels), part.reshape(kv.shape)


def local(query_rows, key_rows, value_rows, cotangent, key_taps, value_taps):
    nz = lax.axis_size("ctx") // 4
    nh = lax.axis_size("head")
    q, cot, kf, vf, kv = gather(
        nz, nh, query_rows, key_rows, value_rows, cotangent, key_taps, value_taps)
    att, gq, part = attention(q, cot, kv)
    return scatter(nz, nh, part, att, gq, kf, vf, key_taps, value_taps)


def solution(mesh):
    rows = P(("ctx", "head"), None)
    taps = P(None, "head")
    return jax.shard_map(
        local,
        mesh=mesh,
        in_specs=(rows, rows, rows, rows, taps, taps),
        out_specs=(rows, rows, rows, rows, taps, taps),
        check_vma=False,
    )
```

```python
import functools

import jax
import jax.numpy as jnp
from jax import lax
from jax.experimental import pallas as pl
from jax.experimental.pallas import tpu as pltpu
from jax.sharding import PartitionSpec as P

D = 1024
HEADS = 16
MESH = pl.DeviceIdType.MESH
F32 = jnp.float32
BF16 = jnp.bfloat16


def place(nz):
    ctx = lax.axis_index("ctx")
    head = lax.axis_index("head")
    core = ctx % 2
    z = (ctx // 2) % nz
    y = ctx // (2 * nz)
    return ctx, head, y, z, core


def ctx_of(nz, y, z, core):
    return (y * nz + z) * 2 + core


def remote(src, dst, send, recv, ctx, head):
    return pltpu.make_async_remote_copy(
        src_ref=src, dst_ref=dst, send_sem=send, recv_sem=recv,
        device_id={"ctx": ctx, "head": head}, device_id_type=MESH,
    )


def greet(sem, ctx, head):
    pl.semaphore_signal(sem, inc=1, device_id={"ctx": ctx, "head": head}, device_id_type=MESH)


def col(h, width):
    return pl.ds(pl.multiple_of(h * width, width), width)


def gather_kernel(nz, nh, q_in, k_in, v_in, cot_in, kt, vt,
                  q_out, cot_out, kf, vf, kv,
                  k_loc, v_loc, halo,
                  a_send, a_recv, a_self, h_send, h_recv,
                  y_send, y_recv, r_send, r_recv, l_send, l_recv, c_send, c_recv):
    ctx, head, y, z, core = place(nz)
    nctx = 4 * nz
    rows = q_in.shape[0]
    ch = q_out.shape[1]
    zr, zl = (z + 1) % nz, (z + nz - 1) % nz
    right, left = ctx_of(nz, y, zr, core), ctx_of(nz, y, zl, core)
    across = ctx_of(nz, 1 - y, z, core)
    mate = ctx_of(nz, y, z, 1 - core)
    last = nh - 1
    gives = (head == last) & (ctx < nctx - 1)
    takes = ctx >= 1

    barrier = pltpu.get_barrier_semaphore()
    for p in range(1, nh):
        greet(barrier, ctx, (head + p) % nh)
    for other in (right, left, across, mate):
        greet(barrier, other, head)

    @pl.when(takes)
    def _():
        greet(barrier, ctx - 1, last)

    @pl.when(gives)
    def _():
        pl.semaphore_wait(barrier, nh - 1 + 4 + nh)

    @pl.when(jnp.logical_not(gives))
    def _():
        pl.semaphore_wait(barrier, nh - 1 + 4)

    pairs = ((k_in, k_loc), (v_in, v_loc), (q_in, q_out), (cot_in, cot_out))

    def halo_copies():
        out = []
        for a in range(2):
            for t in range(nh):
                out.append(remote(
                    pairs[a][0].at[pl.ds(rows - 16, 16), pl.ds(t * ch, ch)], halo.at[a],
                    h_send.at[a, t], h_recv.at[a], ctx + 1, t))
        return out

    def swaps(a):
        out = []
        for p in range(1, nh):
            t = (head + p) % nh
            out.append(remote(
                pairs[a][0].at[:, col(t, ch)], pairs[a][1].at[col(head, rows), :],
                a_send.at[a, p - 1], a_recv.at[a, p - 1], ctx, t))
        return out

    def own(a):
        return pltpu.make_async_copy(
            pairs[a][0].at[:, col(head, ch)], pairs[a][1].at[col(head, rows), :], a_self.at[a])

    moves = [swaps(a) for a in range(4)]
    for a in range(2):
        own(a).start()
        for m in moves[a]:
            m.start()

    @pl.when(gives)
    def _():
        for m in halo_copies():
            m.start()

    @pl.when(jnp.logical_not(takes))
    def _():
        kf[0:8, :] = jnp.zeros((8, ch), F32)
        vf[0:8, :] = jnp.zeros((8, ch), F32)

    @pl.when(takes)
    def _():
        for a, f in ((0, kf), (1, vf)):
            pltpu.make_async_copy(halo.at[a], halo.at[a], h_recv.at[a]).wait()
            f[0:8, :] = halo[a].astype(F32)[8:16, :]

    count = nh * rows // 4
    for a, f, taps in ((0, kf, kt), (1, vf, vt)):
        own(a).wait()
        for m in moves[a]:
            m.wait_recv()
        f[pl.ds(8, nh * rows), :] = pairs[a][1][...].astype(F32)
        packed = (taps[0:1, :] * f[pl.ds(7, count, stride=4), :]
                  + taps[1:2, :] * f[pl.ds(8, count, stride=4), :]
                  + taps[2:3, :] * f[pl.ds(9, count, stride=4), :])
        kv[core, z, pl.ds(pl.multiple_of(y * count, count), count), a * ch:(a + 1) * ch] = packed.astype(BF16)

    def chunk(zz, u):
        side = y + u - 2 * u * y
        return kv.at[core, zz, pl.ds(pl.multiple_of(side * count, count), count), :]

    def to_mate(zz, u, n):
        return remote(chunk(zz, u), chunk(zz, u), c_send.at[n, u], c_recv.at[n, u], mate, head)

    def to_right(s, u):
        here = chunk((z + nz - s) % nz, u)
        return remote(here, here, r_send.at[s, u], r_recv.at[s, u], right, head)

    def to_left(s, u):
        here = chunk((z + s) % nz, u)
        return remote(here, here, l_send.at[s, u], l_recv.at[s, u], left, head)

    nr, nl = nz // 2, nz // 2 - 1
    step_y = remote(chunk(z, 0), chunk(z, 0), y_send, y_recv, across, head)
    step_y.start()
    to_right(0, 0).start()
    to_left(0, 0).start()
    mates = [to_mate(z, 0, 0)]
    mates[0].start()
    for a in range(2, 4):
        own(a).start()
        for m in moves[a]:
            m.start()
    step_y.wait_recv()
    to_right(0, 1).start()
    to_left(0, 1).start()
    mates.append(to_mate(z, 1, 0))
    mates[1].start()
    for s in range(nr):
        for u in range(2):
            to_right(s, u).wait_recv()
            if s + 1 < nr:
                to_right(s + 1, u).start()
            mates.append(to_mate((z + nz - s - 1) % nz, u, 1 + s))
            mates[-1].start()
            if s < nl:
                to_left(s, u).wait_recv()
                if s + 1 < nl:
                    to_left(s + 1, u).start()
                mates.append(to_mate((z + s + 1) % nz, u, 1 + nr + s))
                mates[-1].start()
    for a in range(2, 4):
        own(a).wait()
        for m in moves[a]:
            m.wait_recv()
    for m in mates:
        m.wait()
    for u in range(2):
        for s in range(nr):
            to_right(s, u).wait_send()
        for s in range(nl):
            to_left(s, u).wait_send()
    step_y.wait_send()
    for a in range(4):
        for m in moves[a]:
            m.wait_send()

    @pl.when(gives)
    def _():
        for m in halo_copies():
            m.wait_send()


def gather(nz, nh, q, k, v, cot, kt, vt):
    rows, width = q.shape
    ch = width // nh
    length = nh * rows
    count = length // 4
    vm = pl.BlockSpec(memory_space=pltpu.VMEM)
    dma = pltpu.SemaphoreType.DMA
    return pl.pallas_call(
        functools.partial(gather_kernel, nz, nh),
        out_shape=(
            jax.ShapeDtypeStruct((length, ch), BF16),
            jax.ShapeDtypeStruct((length, ch), BF16),
            jax.ShapeDtypeStruct((length + 8, ch), F32),
            jax.ShapeDtypeStruct((length + 8, ch), F32),
            jax.ShapeDtypeStruct((2, nz, 2 * count, 2 * ch), BF16),
        ),
        in_specs=[pl.BlockSpec(memory_space=pltpu.HBM)] * 4 + [vm] * 2,
        out_specs=(vm,) * 5,
        scratch_shapes=[
            pltpu.VMEM((length, ch), BF16),
            pltpu.VMEM((length, ch), BF16),
            pltpu.VMEM((2, 16, ch), BF16),
            dma((4, nh - 1)), dma((4, nh - 1)), dma((4,)),
            dma((2, nh)), dma((2,)),
            dma(()), dma(()),
            dma((nz // 2, 2)), dma((nz // 2, 2)),
            dma((nz // 2 - 1, 2)), dma((nz // 2 - 1, 2)),
            dma((nz, 2)), dma((nz, 2)),
        ],
        compiler_params=pltpu.CompilerParams(
            collective_id=0, has_side_effects=True, vmem_limit_bytes=40 << 20),
        name="gather",
    )(q, k, v, cot, kt, vt)


def scatter_kernel(nz, nh, part, att_in, gq_in, kf, vf, kt, vt,
                   att_out, gq_out, gk_out, gv_out, kt_out, vt_out,
                   pin, rbuf, rout, lbuf, lout, ybuf, yout, spread, gk_loc, gv_loc,
                   edge, edge_in, tap1, tap2,
                   a_send, a_recv, a_self, e_send, e_recv,
                   y_send, y_recv, r_send, r_recv, l_send, l_recv, c_send, c_recv,
                   t_send, t_recv, u_send, u_recv):
    ctx, head, y, z, core = place(nz)
    nctx = 4 * nz
    rows = att_out.shape[0]
    ch = att_in.shape[1]
    count = nh * rows // 4
    zr, zl = (z + 1) % nz, (z + nz - 1) % nz
    right, left = ctx_of(nz, y, zr, core), ctx_of(nz, y, zl, core)
    across = ctx_of(nz, 1 - y, z, core)
    mate = ctx_of(nz, y, z, 1 - core)
    corner = ctx_of(nz, 1 - y, z, 1 - core)
    last = nh - 1
    takes = (head == last) & (ctx < nctx - 1)
    gives = ctx >= 1

    barrier = pltpu.get_barrier_semaphore()
    for p in range(1, nh):
        greet(barrier, ctx, (head + p) % nh)
    for p in range(1, nz):
        greet(barrier, ctx_of(nz, y, (z + p) % nz, core), head)
    for other in (across, mate, corner):
        greet(barrier, other, head)

    @pl.when(takes)
    def _():
        for t in range(nh):
            greet(barrier, ctx + 1, t)

    @pl.when(gives)
    def _():
        pl.semaphore_wait(barrier, nh - 1 + nz - 1 + 3 + 1)

    @pl.when(jnp.logical_not(gives))
    def _():
        pl.semaphore_wait(barrier, nh - 1 + nz - 1 + 3)

    nr, nl = nz // 2, nz // 2 - 1

    def to_mate(zz, n):
        return remote(part.at[1 - core, zz], pin.at[zz], c_send.at[n], c_recv.at[n], mate, head)

    order = []
    for s in range(nr):
        order.append((z + nz // 2 + nz - s) % nz)
        if s < nl:
            order.append((z + nz - nl + s) % nz)
    order.append(z)
    mates = [to_mate(zz, n) for n, zz in enumerate(order)]
    for m in mates:
        m.start()

    pairs = ((att_in, att_out), (gq_in, gq_out), (gk_loc, gk_out), (gv_loc, gv_out))

    def swaps(a):
        out = []
        for p in range(1, nh):
            t = (head + p) % nh
            out.append(remote(
                pairs[a][0].at[col(t, rows), :], pairs[a][1].at[:, col(head, ch)],
                a_send.at[a, p - 1], a_recv.at[a, p - 1], ctx, t))
        return out

    def own(a):
        return pltpu.make_async_copy(
            pairs[a][0].at[col(head, rows), :], pairs[a][1].at[:, col(head, ch)], a_self.at[a])

    moves = [swaps(a) for a in range(4)]
    for a in range(2):
        own(a).start()
        for m in moves[a]:
            m.start()

    def part_of(u):
        side = 1 - y - u + 2 * u * y
        return pl.ds(pl.multiple_of(side * count, count), count)

    def local_sum(n, u):
        if u == 0:
            mates[n].wait_recv()
        zz = order[n]
        return part[core, zz, part_of(u), :].astype(F32) + pin[zz, part_of(u), :].astype(F32)

    def to_right(s, u):
        return remote(rout.at[s, u], rbuf.at[s, u], r_send.at[s, u], r_recv.at[s, u], right, head)

    def to_left(s, u):
        return remote(lout.at[s, u], lbuf.at[s, u], l_send.at[s, u], l_recv.at[s, u], left, head)

    for s in range(nr):
        for u in range(2):
            n = 2 * s
            total = local_sum(n, u)
            if s > 0:
                to_right(s - 1, u).wait_recv()
                total = total + rbuf[s - 1, u].astype(F32)
            rout[s, u] = total.astype(BF16)
            to_right(s, u).start()
            if s < nl:
                total = local_sum(n + 1, u)
                if s > 0:
                    to_left(s - 1, u).wait_recv()
                    total = total + lbuf[s - 1, u].astype(F32)
                lout[s, u] = total.astype(BF16)
                to_left(s, u).start()
    for u in range(2):
        total = local_sum(2 * nr - 1, u)
        to_left(nl - 1, u).wait_recv()
        total = total + lbuf[nl - 1, u].astype(F32)
        to_right(nr - 1, u).wait_recv()
        total = total + rbuf[nr - 1, u].astype(F32)
        if u == 0:
            ybuf[...] = total.astype(BF16)
            step_y = remote(ybuf, yout, y_send, y_recv, across, head)
            step_y.start()
        else:
            step_y.wait_recv()
            grads = total + yout[...].astype(F32)

    tap1[z, 6:8, :] = jnp.zeros((2, ch), F32)
    for a, f, taps, loc in ((0, kf, kt, gk_loc), (1, vf, vt, gv_loc)):
        g = grads[:, a * ch:(a + 1) * ch]
        spread[a, 0:8, :] = jnp.zeros((8, ch), F32)
        spread[a, pl.ds(nh * rows, 8), :] = jnp.zeros((8, ch), F32)
        spread[a, pl.ds(7, count, stride=4), :] = taps[0:1, :] * g
        spread[a, pl.ds(8, count, stride=4), :] = taps[1:2, :] * g
        spread[a, pl.ds(9, count, stride=4), :] = taps[2:3, :] * g
        spread[a, pl.ds(10, count, stride=4), :] = jnp.zeros((count, ch), F32)
        spread[a, pl.ds(nh * rows + 7, 1), :] = jnp.zeros((1, ch), F32)
        loc[...] = spread[a, pl.ds(8, nh * rows), :].astype(BF16)
        edge[a] = jnp.concatenate([jnp.zeros((8, ch), F32), spread[a, 0:8, :]], axis=0).astype(BF16)
        for t in range(3):
            tap1[z, 3 * a + t:3 * a + t + 1, :] = jnp.sum(
                g * f[pl.ds(7 + t, count, stride=4), :], axis=0, keepdims=True)

    def tap_z():
        out = []
        for p in range(1, nz):
            out.append(remote(tap1.at[z], tap1.at[z], t_send.at[p - 1], t_recv.at[p - 1],
                              ctx_of(nz, y, (z + p) % nz, core), head))
        return out

    def tap_yc():
        out = []
        for m, other in enumerate((across, mate, corner)):
            spot = tap2.at[2 * y + core]
            out.append(remote(spot, spot, u_send.at[m], u_recv.at[m], other, head))
        return out

    def edges():
        return [remote(edge.at[a], edge_in.at[a, head], e_send.at[a], e_recv.at[a, head],
                       ctx - 1, last) for a in range(2)]

    for m in tap_z():
        m.start()

    @pl.when(gives)
    def _():
        for m in edges():
            m.start()

    for a in range(2, 4):
        own(a).start()
        for m in moves[a]:
            m.start()

    for m in tap_z():
        m.wait_recv()
    total = tap1[0]
    for i in range(1, nz):
        total = total + tap1[i]
    tap2[2 * y + core] = total
    for m in tap_yc():
        m.start()

    for a in range(4):
        own(a).wait()
        for m in moves[a]:
            m.wait_recv()

    @pl.when(takes)
    def _():
        for a in range(2):
            for t in range(nh):
                pltpu.make_async_copy(edge_in.at[a, t], edge_in.at[a, t], e_recv.at[a, t]).wait()
                spot = (pl.ds(rows - 16, 16), pl.ds(t * ch, ch))
                out = pairs[2 + a][1]
                out[spot] = (out[spot].astype(F32) + edge_in[a, t].astype(F32)).astype(BF16)

    for m in tap_yc():
        m.wait_recv()
    total = (tap2[0] + tap2[1]) + (tap2[2] + tap2[3])
    kt_out[...] = total[0:3, :]
    vt_out[...] = total[3:6, :]

    for m in mates:
        m.wait_send()
    for u in range(2):
        for s in range(nr):
            to_right(s, u).wait_send()
        for s in range(nl):
            to_left(s, u).wait_send()
    step_y.wait_send()
    for a in range(4):
        for m in moves[a]:
            m.wait_send()
    for m in tap_z():
        m.wait_send()
    for m in tap_yc():
        m.wait_send()

    @pl.when(gives)
    def _():
        for m in edges():
            m.wait_send()


def scatter(nz, nh, part, att, gq, kf, vf, kt, vt):
    length, ch = att.shape
    rows = length // nh
    count = length // 4
    vm = pl.BlockSpec(memory_space=pltpu.VMEM)
    dma = pltpu.SemaphoreType.DMA
    nr, nl = nz // 2, nz // 2 - 1
    wide = jax.ShapeDtypeStruct((rows, nh * ch), BF16)
    small = jax.ShapeDtypeStruct((3, ch), F32)
    return pl.pallas_call(
        functools.partial(scatter_kernel, nz, nh),
        out_shape=(wide, wide, wide, wide, small, small),
        in_specs=[vm] * 7,
        out_specs=(vm,) * 6,
        scratch_shapes=[
            pltpu.VMEM((nz, 2 * count, 2 * ch), BF16),
            pltpu.VMEM((nr, 2, count, 2 * ch), BF16),
            pltpu.VMEM((nr, 2, count, 2 * ch), BF16),
            pltpu.VMEM((nl, 2, count, 2 * ch), BF16),
            pltpu.VMEM((nl, 2, count, 2 * ch), BF16),
            pltpu.VMEM((count, 2 * ch), BF16),
            pltpu.VMEM((count, 2 * ch), BF16),
            pltpu.VMEM((2, length + 16, ch), F32),
            pltpu.VMEM((length, ch), BF16),
            pltpu.VMEM((length, ch), BF16),
            pltpu.VMEM((2, 16, ch), BF16),
            pltpu.VMEM((2, nh, 16, ch), BF16),
            pltpu.VMEM((nz, 8, ch), F32),
            pltpu.VMEM((4, 8, ch), F32),
            dma((4, nh - 1)), dma((4, nh - 1)), dma((4,)),
            dma((2,)), dma((2, nh)),
            dma(()), dma(()),
            dma((nr, 2)), dma((nr, 2)),
            dma((nl, 2)), dma((nl, 2)),
            dma((nz,)), dma((nz,)),
            dma((nz - 1,)), dma((nz - 1,)),
            dma((3,)), dma((3,)),
        ],
        compiler_params=pltpu.CompilerParams(
            collective_id=1, has_side_effects=True, vmem_limit_bytes=40 << 20),
        name="scatter",
    )(part, att, gq, kf, vf, kt, vt)


def attention(q, cot, kv):
    length, channels = q.shape
    head_dim = D // HEADS
    heads = channels // head_dim
    scaling = head_dim ** (-0.5)
    flat = kv.reshape(-1, 2 * channels)
    qh = q.reshape(length, heads, head_dim)
    ch = cot.reshape(length, heads, head_dim)
    kh = flat[:, :channels].reshape(-1, heads, head_dim)
    vh = flat[:, channels:].reshape(-1, heads, head_dim)
    scores = jnp.einsum("qhd,khd->hqk", qh, kh, preferred_element_type=F32) * scaling
    raised = jnp.exp(scores - jnp.max(scores, axis=2, keepdims=True))
    weights = (raised / jnp.sum(raised, axis=2, keepdims=True)).astype(BF16)
    att = jnp.einsum("hqk,khd->qhd", weights, vh, preferred_element_type=F32).astype(BF16)
    offset = jnp.sum(ch.astype(F32) * att.astype(F32), axis=2)
    dweights = jnp.einsum("qhd,khd->hqk", ch, vh, preferred_element_type=F32)
    dscores = (weights.astype(F32) * (dweights - offset.T[:, :, None])).astype(BF16)
    gq = (jnp.einsum("hqk,khd->qhd", dscores, kh, preferred_element_type=F32) * scaling).astype(BF16)
    gk = jnp.einsum("hqk,qhd->khd", dscores, qh, preferred_element_type=F32) * scaling
    gv = jnp.einsum("hqk,qhd->khd", weights, ch, preferred_element_type=F32)
    part = jnp.concatenate(
        [gk.reshape(-1, channels), gv.reshape(-1, channels)], axis=1).astype(BF16)
    return att.reshape(length, channels), gq.reshape(length, channels), part.reshape(kv.shape)


def local(query_rows, key_rows, value_rows, cotangent, key_taps, value_taps):
    nz = lax.axis_size("ctx") // 4
    nh = lax.axis_size("head")
    q, cot, kf, vf, kv = gather(
        nz, nh, query_rows, key_rows, value_rows, cotangent, key_taps, value_taps)
    att, gq, part = attention(q, cot, kv)
    return scatter(nz, nh, part, att, gq, kf, vf, key_taps, value_taps)


def solution(mesh):
    rows = P(("ctx", "head"), None)
    taps = P(None, "head")
    return jax.shard_map(
        local,
        mesh=mesh,
        in_specs=(rows, rows, rows, rows, taps, taps),
        out_specs=(rows, rows, rows, rows, taps, taps),
        check_vma=False,
    )
```

```python
import functools

import jax
import jax.numpy as jnp
from jax import lax
from jax.experimental import pallas as pl
from jax.experimental.pallas import tpu as pltpu
from jax.sharding import PartitionSpec as P

MESH = pl.DeviceIdType.MESH
F32 = jnp.float32
BF16 = jnp.bfloat16


def place(nz):
    ctx = lax.axis_index("ctx")
    head = lax.axis_index("head")
    core = ctx % 2
    z = (ctx // 2) % nz
    y = ctx // (2 * nz)
    return ctx, head, y, z, core


def ctx_of(nz, y, z, core):
    return (y * nz + z) * 2 + core


def remote(src, dst, send, recv, ctx, head):
    return pltpu.make_async_remote_copy(
        src_ref=src, dst_ref=dst, send_sem=send, recv_sem=recv,
        device_id={"ctx": ctx, "head": head}, device_id_type=MESH,
    )


def greet(sem, ctx, head):
    pl.semaphore_signal(sem, inc=1, device_id={"ctx": ctx, "head": head}, device_id_type=MESH)


def col(h, width):
    return pl.ds(pl.multiple_of(h * width, width), width)


def gather_kernel(nz, nh, q_in, k_in, v_in, cot_in, kt, vt,
                  q_out, cot_out, kf, vf, kv,
                  k_loc, v_loc, halo,
                  a_send, a_recv, a_self, h_send, h_recv,
                  y_send, y_recv, r_send, r_recv, l_send, l_recv, c_send, c_recv):
    ctx, head, y, z, core = place(nz)
    nctx = 4 * nz
    rows = q_in.shape[0]
    ch = q_out.shape[1]
    zr, zl = (z + 1) % nz, (z + nz - 1) % nz
    right, left = ctx_of(nz, y, zr, core), ctx_of(nz, y, zl, core)
    across = ctx_of(nz, 1 - y, z, core)
    mate = ctx_of(nz, y, z, 1 - core)
    last = nh - 1
    gives = (head == last) & (ctx < nctx - 1)
    takes = ctx >= 1

    barrier = pltpu.get_barrier_semaphore()
    for p in range(1, nh):
        greet(barrier, ctx, (head + p) % nh)
    for other in (right, left, across, mate):
        greet(barrier, other, head)

    @pl.when(takes)
    def _():
        greet(barrier, ctx - 1, last)

    @pl.when(gives)
    def _():
        pl.semaphore_wait(barrier, nh - 1 + 4 + nh)

    @pl.when(jnp.logical_not(gives))
    def _():
        pl.semaphore_wait(barrier, nh - 1 + 4)

    pairs = ((k_in, k_loc), (v_in, v_loc), (q_in, q_out), (cot_in, cot_out))

    def halo_copies():
        out = []
        for a in range(2):
            for t in range(nh):
                out.append(remote(
                    pairs[a][0].at[pl.ds(rows - 16, 16), pl.ds(t * ch, ch)], halo.at[a],
                    h_send.at[a, t], h_recv.at[a], ctx + 1, t))
        return out

    def swaps(a):
        out = []
        for p in range(1, nh):
            t = (head + p) % nh
            out.append(remote(
                pairs[a][0].at[:, col(t, ch)], pairs[a][1].at[col(head, rows), :],
                a_send.at[a, p - 1], a_recv.at[a, p - 1], ctx, t))
        return out

    def own(a):
        return pltpu.make_async_copy(
            pairs[a][0].at[:, col(head, ch)], pairs[a][1].at[col(head, rows), :], a_self.at[a])

    moves = [swaps(a) for a in range(4)]
    for a in range(2):
        own(a).start()
        for m in moves[a]:
            m.start()

    @pl.when(gives)
    def _():
        for m in halo_copies():
            m.start()

    @pl.when(jnp.logical_not(takes))
    def _():
        kf[0:8, :] = jnp.zeros((8, ch), F32)
        vf[0:8, :] = jnp.zeros((8, ch), F32)

    @pl.when(takes)
    def _():
        for a, f in ((0, kf), (1, vf)):
            pltpu.make_async_copy(halo.at[a], halo.at[a], h_recv.at[a]).wait()
            f[0:8, :] = halo[a].astype(F32)[8:16, :]

    count = nh * rows // 4
    for a, f, taps in ((0, kf, kt), (1, vf, vt)):
        own(a).wait()
        for m in moves[a]:
            m.wait_recv()
        f[pl.ds(8, nh * rows), :] = pairs[a][1][...].astype(F32)
        packed = (taps[0:1, :] * f[pl.ds(7, count, stride=4), :]
                  + taps[1:2, :] * f[pl.ds(8, count, stride=4), :]
                  + taps[2:3, :] * f[pl.ds(9, count, stride=4), :])
        kv[core, z, pl.ds(pl.multiple_of(y * count, count), count), a * ch:(a + 1) * ch] = packed.astype(BF16)

    def chunk(zz, u):
        side = y + u - 2 * u * y
        return kv.at[core, zz, pl.ds(pl.multiple_of(side * count, count), count), :]

    def to_mate(zz, u, n):
        return remote(chunk(zz, u), chunk(zz, u), c_send.at[n, u], c_recv.at[n, u], mate, head)

    def to_right(s, u):
        here = chunk((z + nz - s) % nz, u)
        return remote(here, here, r_send.at[s, u], r_recv.at[s, u], right, head)

    def to_left(s, u):
        here = chunk((z + s) % nz, u)
        return remote(here, here, l_send.at[s, u], l_recv.at[s, u], left, head)

    nr, nl = nz // 2, nz // 2 - 1
    step_y = remote(chunk(z, 0), chunk(z, 0), y_send, y_recv, across, head)
    step_y.start()
    to_right(0, 0).start()
    to_left(0, 0).start()
    mates = [to_mate(z, 0, 0)]
    mates[0].start()
    for a in range(2, 4):
        own(a).start()
        for m in moves[a]:
            m.start()
    step_y.wait_recv()
    to_right(0, 1).start()
    to_left(0, 1).start()
    mates.append(to_mate(z, 1, 0))
    mates[1].start()
    for s in range(nr):
        for u in range(2):
            to_right(s, u).wait_recv()
            if s + 1 < nr:
                to_right(s + 1, u).start()
            mates.append(to_mate((z + nz - s - 1) % nz, u, 1 + s))
            mates[-1].start()
            if s < nl:
                to_left(s, u).wait_recv()
                if s + 1 < nl:
                    to_left(s + 1, u).start()
                mates.append(to_mate((z + s + 1) % nz, u, 1 + nr + s))
                mates[-1].start()
    for a in range(2, 4):
        own(a).wait()
        for m in moves[a]:
            m.wait_recv()
    for m in mates:
        m.wait()
    for u in range(2):
        for s in range(nr):
            to_right(s, u).wait_send()
        for s in range(nl):
            to_left(s, u).wait_send()
    step_y.wait_send()
    for a in range(4):
        for m in moves[a]:
            m.wait_send()

    @pl.when(gives)
    def _():
        for m in halo_copies():
            m.wait_send()


def gather(nz, nh, q, k, v, cot, kt, vt):
    rows, width = q.shape
    ch = width // nh
    length = nh * rows
    count = length // 4
    vm = pl.BlockSpec(memory_space=pltpu.VMEM)
    dma = pltpu.SemaphoreType.DMA
    return pl.pallas_call(
        functools.partial(gather_kernel, nz, nh),
        out_shape=(
            jax.ShapeDtypeStruct((length, ch), BF16),
            jax.ShapeDtypeStruct((length, ch), BF16),
            jax.ShapeDtypeStruct((length + 8, ch), F32),
            jax.ShapeDtypeStruct((length + 8, ch), F32),
            jax.ShapeDtypeStruct((2, nz, 2 * count, 2 * ch), BF16),
        ),
        in_specs=[pl.BlockSpec(memory_space=pltpu.HBM)] * 4 + [vm] * 2,
        out_specs=(vm,) * 5,
        scratch_shapes=[
            pltpu.VMEM((length, ch), BF16),
            pltpu.VMEM((length, ch), BF16),
            pltpu.VMEM((2, 16, ch), BF16),
            dma((4, nh - 1)), dma((4, nh - 1)), dma((4,)),
            dma((2, nh)), dma((2,)),
            dma(()), dma(()),
            dma((nz // 2, 2)), dma((nz // 2, 2)),
            dma((nz // 2 - 1, 2)), dma((nz // 2 - 1, 2)),
            dma((nz, 2)), dma((nz, 2)),
        ],
        compiler_params=pltpu.CompilerParams(
            collective_id=0, has_side_effects=True, vmem_limit_bytes=40 << 20),
        name="gather",
    )(q, k, v, cot, kt, vt)


def scatter_kernel(nz, nh, part, att_in, gq_in, kf, vf, kt, vt,
                   att_out, gq_out, gk_out, gv_out, kt_out, vt_out,
                   pin, rbuf, rout, lbuf, lout, ybuf, yout, spread, gk_loc, gv_loc,
                   edge, edge_in, tap1, tap2,
                   a_send, a_recv, a_self, e_send, e_recv,
                   y_send, y_recv, r_send, r_recv, l_send, l_recv, c_send, c_recv,
                   t_send, t_recv, u_send, u_recv):
    ctx, head, y, z, core = place(nz)
    nctx = 4 * nz
    rows = att_out.shape[0]
    ch = att_in.shape[1]
    count = nh * rows // 4
    zr, zl = (z + 1) % nz, (z + nz - 1) % nz
    right, left = ctx_of(nz, y, zr, core), ctx_of(nz, y, zl, core)
    across = ctx_of(nz, 1 - y, z, core)
    mate = ctx_of(nz, y, z, 1 - core)
    corner = ctx_of(nz, 1 - y, z, 1 - core)
    last = nh - 1
    takes = (head == last) & (ctx < nctx - 1)
    gives = ctx >= 1

    barrier = pltpu.get_barrier_semaphore()
    for p in range(1, nh):
        greet(barrier, ctx, (head + p) % nh)
    for p in range(1, nz):
        greet(barrier, ctx_of(nz, y, (z + p) % nz, core), head)
    for other in (across, mate, corner):
        greet(barrier, other, head)

    @pl.when(takes)
    def _():
        for t in range(nh):
            greet(barrier, ctx + 1, t)

    @pl.when(gives)
    def _():
        pl.semaphore_wait(barrier, nh - 1 + nz - 1 + 3 + 1)

    @pl.when(jnp.logical_not(gives))
    def _():
        pl.semaphore_wait(barrier, nh - 1 + nz - 1 + 3)

    nr, nl = nz // 2, nz // 2 - 1

    def to_mate(zz, n):
        return remote(part.at[1 - core, zz], pin.at[zz], c_send.at[n], c_recv.at[n], mate, head)

    order = []
    for s in range(nr):
        order.append((z + nz // 2 + nz - s) % nz)
        if s < nl:
            order.append((z + nz - nl + s) % nz)
    order.append(z)
    mates = [to_mate(zz, n) for n, zz in enumerate(order)]
    for m in mates:
        m.start()

    pairs = ((att_in, att_out), (gq_in, gq_out), (gk_loc, gk_out), (gv_loc, gv_out))

    def swaps(a):
        out = []
        for p in range(1, nh):
            t = (head + p) % nh
            out.append(remote(
                pairs[a][0].at[col(t, rows), :], pairs[a][1].at[:, col(head, ch)],
                a_send.at[a, p - 1], a_recv.at[a, p - 1], ctx, t))
        return out

    def own(a):
        return pltpu.make_async_copy(
            pairs[a][0].at[col(head, rows), :], pairs[a][1].at[:, col(head, ch)], a_self.at[a])

    moves = [swaps(a) for a in range(4)]
    for a in range(2):
        own(a).start()
        for m in moves[a]:
            m.start()

    def part_of(u):
        side = 1 - y - u + 2 * u * y
        return pl.ds(pl.multiple_of(side * count, count), count)

    def local_sum(n, u):
        if u == 0:
            mates[n].wait_recv()
        zz = order[n]
        return part[core, zz, part_of(u), :].astype(F32) + pin[zz, part_of(u), :].astype(F32)

    def to_right(s, u):
        return remote(rout.at[s, u], rbuf.at[s, u], r_send.at[s, u], r_recv.at[s, u], right, head)

    def to_left(s, u):
        return remote(lout.at[s, u], lbuf.at[s, u], l_send.at[s, u], l_recv.at[s, u], left, head)

    for s in range(nr):
        for u in range(2):
            n = 2 * s
            total = local_sum(n, u)
            if s > 0:
                to_right(s - 1, u).wait_recv()
                total = total + rbuf[s - 1, u].astype(F32)
            rout[s, u] = total.astype(BF16)
            to_right(s, u).start()
            if s < nl:
                total = local_sum(n + 1, u)
                if s > 0:
                    to_left(s - 1, u).wait_recv()
                    total = total + lbuf[s - 1, u].astype(F32)
                lout[s, u] = total.astype(BF16)
                to_left(s, u).start()
    for u in range(2):
        total = local_sum(2 * nr - 1, u)
        to_left(nl - 1, u).wait_recv()
        total = total + lbuf[nl - 1, u].astype(F32)
        to_right(nr - 1, u).wait_recv()
        total = total + rbuf[nr - 1, u].astype(F32)
        if u == 0:
            ybuf[...] = total.astype(BF16)
            step_y = remote(ybuf, yout, y_send, y_recv, across, head)
            step_y.start()
        else:
            step_y.wait_recv()
            grads = total + yout[...].astype(F32)

    tap1[z, 6:8, :] = jnp.zeros((2, ch), F32)
    for a, f, taps, loc in ((0, kf, kt, gk_loc), (1, vf, vt, gv_loc)):
        g = grads[:, a * ch:(a + 1) * ch]
        spread[a, 0:8, :] = jnp.zeros((8, ch), F32)
        spread[a, pl.ds(nh * rows, 8), :] = jnp.zeros((8, ch), F32)
        spread[a, pl.ds(7, count, stride=4), :] = taps[0:1, :] * g
        spread[a, pl.ds(8, count, stride=4), :] = taps[1:2, :] * g
        spread[a, pl.ds(9, count, stride=4), :] = taps[2:3, :] * g
        spread[a, pl.ds(10, count, stride=4), :] = jnp.zeros((count, ch), F32)
        spread[a, pl.ds(nh * rows + 7, 1), :] = jnp.zeros((1, ch), F32)
        loc[...] = spread[a, pl.ds(8, nh * rows), :].astype(BF16)
        edge[a] = jnp.concatenate([jnp.zeros((8, ch), F32), spread[a, 0:8, :]], axis=0).astype(BF16)
        for t in range(3):
            tap1[z, 3 * a + t:3 * a + t + 1, :] = jnp.sum(
                g * f[pl.ds(7 + t, count, stride=4), :], axis=0, keepdims=True)

    def tap_z():
        out = []
        for p in range(1, nz):
            out.append(remote(tap1.at[z], tap1.at[z], t_send.at[p - 1], t_recv.at[p - 1],
                              ctx_of(nz, y, (z + p) % nz, core), head))
        return out

    def tap_yc():
        out = []
        for m, other in enumerate((across, mate, corner)):
            spot = tap2.at[2 * y + core]
            out.append(remote(spot, spot, u_send.at[m], u_recv.at[m], other, head))
        return out

    def edges():
        return [remote(edge.at[a], edge_in.at[a, head], e_send.at[a], e_recv.at[a, head],
                       ctx - 1, last) for a in range(2)]

    for m in tap_z():
        m.start()

    @pl.when(gives)
    def _():
        for m in edges():
            m.start()

    for a in range(2, 4):
        own(a).start()
        for m in moves[a]:
            m.start()

    for m in tap_z():
        m.wait_recv()
    total = tap1[0]
    for i in range(1, nz):
        total = total + tap1[i]
    tap2[2 * y + core] = total
    for m in tap_yc():
        m.start()

    for a in range(4):
        own(a).wait()
        for m in moves[a]:
            m.wait_recv()

    @pl.when(takes)
    def _():
        for a in range(2):
            for t in range(nh):
                pltpu.make_async_copy(edge_in.at[a, t], edge_in.at[a, t], e_recv.at[a, t]).wait()
                spot = (pl.ds(rows - 16, 16), pl.ds(t * ch, ch))
                out = pairs[2 + a][1]
                out[spot] = (out[spot].astype(F32) + edge_in[a, t].astype(F32)).astype(BF16)

    for m in tap_yc():
        m.wait_recv()
    total = (tap2[0] + tap2[1]) + (tap2[2] + tap2[3])
    kt_out[...] = total[0:3, :]
    vt_out[...] = total[3:6, :]

    for m in mates:
        m.wait_send()
    for u in range(2):
        for s in range(nr):
            to_right(s, u).wait_send()
        for s in range(nl):
            to_left(s, u).wait_send()
    step_y.wait_send()
    for a in range(4):
        for m in moves[a]:
            m.wait_send()
    for m in tap_z():
        m.wait_send()
    for m in tap_yc():
        m.wait_send()

    @pl.when(gives)
    def _():
        for m in edges():
            m.wait_send()


def scatter(nz, nh, part, att, gq, kf, vf, kt, vt):
    length, ch = att.shape
    rows = length // nh
    count = length // 4
    vm = pl.BlockSpec(memory_space=pltpu.VMEM)
    dma = pltpu.SemaphoreType.DMA
    nr, nl = nz // 2, nz // 2 - 1
    wide = jax.ShapeDtypeStruct((rows, nh * ch), BF16)
    small = jax.ShapeDtypeStruct((3, ch), F32)
    return pl.pallas_call(
        functools.partial(scatter_kernel, nz, nh),
        out_shape=(wide, wide, wide, wide, small, small),
        in_specs=[vm] * 7,
        out_specs=(vm,) * 6,
        scratch_shapes=[
            pltpu.VMEM((nz, 2 * count, 2 * ch), BF16),
            pltpu.VMEM((nr, 2, count, 2 * ch), BF16),
            pltpu.VMEM((nr, 2, count, 2 * ch), BF16),
            pltpu.VMEM((nl, 2, count, 2 * ch), BF16),
            pltpu.VMEM((nl, 2, count, 2 * ch), BF16),
            pltpu.VMEM((count, 2 * ch), BF16),
            pltpu.VMEM((count, 2 * ch), BF16),
            pltpu.VMEM((2, length + 16, ch), F32),
            pltpu.VMEM((length, ch), BF16),
            pltpu.VMEM((length, ch), BF16),
            pltpu.VMEM((2, 16, ch), BF16),
            pltpu.VMEM((2, nh, 16, ch), BF16),
            pltpu.VMEM((nz, 8, ch), F32),
            pltpu.VMEM((4, 8, ch), F32),
            dma((4, nh - 1)), dma((4, nh - 1)), dma((4,)),
            dma((2,)), dma((2, nh)),
            dma(()), dma(()),
            dma((nr, 2)), dma((nr, 2)),
            dma((nl, 2)), dma((nl, 2)),
            dma((nz,)), dma((nz,)),
            dma((nz - 1,)), dma((nz - 1,)),
            dma((3,)), dma((3,)),
        ],
        compiler_params=pltpu.CompilerParams(
            collective_id=1, has_side_effects=True, vmem_limit_bytes=40 << 20),
        name="scatter",
    )(part, att, gq, kf, vf, kt, vt)


def attention_kernel(block, q_ref, cot_ref, kv_ref, att_ref, gq_ref, part_ref,
                     s_ref, e_ref, att_t, gq_t):
    length, ch = q_ref.shape
    half = ch // 2
    keys = kv_ref.shape[0]
    steps = keys // block
    scaling = half ** (-0.5)
    lanes = lax.broadcasted_iota(jnp.int32, (length, ch), 1)

    def split(x):
        x = x.astype(F32)
        zero = jnp.zeros_like(x)
        return jnp.concatenate(
            [jnp.where(lanes < half, x, zero), jnp.where(lanes < half, zero, x)], axis=0).astype(BF16)

    def dot(a, b, ca, cb):
        return lax.dot_general(a, b, (((ca,), (cb,)), ((), ())), preferred_element_type=F32)

    qs = split(q_ref[...].astype(F32) * scaling)
    cots = split(cot_ref[...])

    def at(i):
        return pl.ds(pl.multiple_of(i * block, block), block)

    def scores(i, top):
        s = dot(kv_ref[at(i), 0:ch], qs, 1, 1)
        s_ref[at(i), :] = s
        return jnp.maximum(top, jnp.max(s.reshape(block // 8, 8, 2 * length), axis=0))

    top = lax.fori_loop(0, steps, scores, jnp.full((8, 2 * length), -jnp.inf, F32))
    top = jnp.max(top, axis=0, keepdims=True)

    att_t[...] = jnp.zeros_like(att_t)
    gq_t[...] = jnp.zeros_like(gq_t)

    def raise_(i, total):
        e = jnp.exp(s_ref[at(i), :] - top)
        eb = e.astype(BF16)
        e_ref[at(i), :] = eb
        att_t[...] += dot(kv_ref[at(i), ch:2 * ch], eb, 0, 0)
        return total + jnp.sum(e.reshape(block // 8, 8, 2 * length), axis=0)

    total = lax.fori_loop(0, steps, raise_, jnp.zeros((8, 2 * length), F32))
    inv = 1.0 / jnp.sum(total, axis=0, keepdims=True)

    def join(x):
        return jnp.concatenate([x[0:half, 0:length], x[half:ch, length:2 * length]], axis=0)

    att = jnp.transpose(join(att_t[...] * inv)).astype(BF16)
    att_ref[...] = att
    prod = jnp.transpose(cot_ref[...].astype(F32) * att.astype(F32))
    offset = jnp.concatenate(
        [jnp.sum(prod[0:half], axis=0, keepdims=True),
         jnp.sum(prod[half:ch], axis=0, keepdims=True)], axis=1)

    def back(i, carry):
        w = e_ref[at(i), :].astype(F32) * inv
        dw = dot(kv_ref[at(i), ch:2 * ch], cots, 1, 1)
        ds = (w * (dw - offset)).astype(BF16)
        part_ref[at(i), 0:ch] = dot(ds, qs, 1, 0).astype(BF16)
        part_ref[at(i), ch:2 * ch] = dot(w.astype(BF16), cots, 1, 0).astype(BF16)
        gq_t[...] += dot(kv_ref[at(i), 0:ch], ds, 0, 0)
        return carry

    lax.fori_loop(0, steps, back, 0)
    gq_ref[...] = (jnp.transpose(join(gq_t[...])) * scaling).astype(BF16)


def attention(q, cot, kv):
    length, ch = q.shape
    flat = kv.reshape(-1, 2 * ch)
    keys = flat.shape[0]
    vm = pl.BlockSpec(memory_space=pltpu.VMEM)
    att, gq, part = pl.pallas_call(
        functools.partial(attention_kernel, 512),
        out_shape=(
            jax.ShapeDtypeStruct((length, ch), BF16),
            jax.ShapeDtypeStruct((length, ch), BF16),
            jax.ShapeDtypeStruct((keys, 2 * ch), BF16),
        ),
        in_specs=[vm] * 3,
        out_specs=(vm,) * 3,
        scratch_shapes=[
            pltpu.VMEM((keys, 2 * length), F32),
            pltpu.VMEM((keys, 2 * length), BF16),
            pltpu.VMEM((ch, 2 * length), F32),
            pltpu.VMEM((ch, 2 * length), F32),
        ],
        compiler_params=pltpu.CompilerParams(vmem_limit_bytes=48 << 20),
        name="attention",
    )(q, cot, flat)
    return att, gq, part.reshape(kv.shape)


def local(query_rows, key_rows, value_rows, cotangent, key_taps, value_taps):
    nz = lax.axis_size("ctx") // 4
    nh = lax.axis_size("head")
    q, cot, kf, vf, kv = gather(
        nz, nh, query_rows, key_rows, value_rows, cotangent, key_taps, value_taps)
    att, gq, part = attention(q, cot, kv)
    return scatter(nz, nh, part, att, gq, kf, vf, key_taps, value_taps)


def solution(mesh):
    rows = P(("ctx", "head"), None)
    taps = P(None, "head")
    return jax.shard_map(
        local,
        mesh=mesh,
        in_specs=(rows, rows, rows, rows, taps, taps),
        out_specs=(rows, rows, rows, rows, taps, taps),
        check_vma=False,
    )
```

```python
import functools

import jax
import jax.numpy as jnp
from jax import lax
from jax.experimental import pallas as pl
from jax.experimental.pallas import tpu as pltpu
from jax.sharding import PartitionSpec as P

MESH = pl.DeviceIdType.MESH
F32 = jnp.float32
JUMP = 5
BF16 = jnp.bfloat16


def place(nz):
    ctx = lax.axis_index("ctx")
    head = lax.axis_index("head")
    core = ctx % 2
    z = (ctx // 2) % nz
    y = ctx // (2 * nz)
    return ctx, head, y, z, core


def ctx_of(nz, y, z, core):
    return (y * nz + z) * 2 + core


def remote(src, dst, send, recv, ctx, head):
    return pltpu.make_async_remote_copy(
        src_ref=src, dst_ref=dst, send_sem=send, recv_sem=recv,
        device_id={"ctx": ctx, "head": head}, device_id_type=MESH,
    )


def greet(sem, ctx, head):
    pl.semaphore_signal(sem, inc=1, device_id={"ctx": ctx, "head": head}, device_id_type=MESH)


def col(h, width):
    return pl.ds(pl.multiple_of(h * width, width), width)


def gather_kernel(nz, nh, q_in, k_in, v_in, cot_in, kt, vt,
                  q_out, cot_out, kf, vf, kv,
                  k_loc, v_loc, halo,
                  a_send, a_recv, a_self, h_send, h_recv,
                  y_send, y_recv, r_send, r_recv, l_send, l_recv, c_send, c_recv, j_send, j_recv):
    ctx, head, y, z, core = place(nz)
    nctx = 4 * nz
    rows = q_in.shape[0]
    ch = q_out.shape[1]
    zr, zl = (z + 1) % nz, (z + nz - 1) % nz
    right, left = ctx_of(nz, y, zr, core), ctx_of(nz, y, zl, core)
    across = ctx_of(nz, 1 - y, z, core)
    mate = ctx_of(nz, y, z, 1 - core)
    last = nh - 1
    gives = (head == last) & (ctx < nctx - 1)
    takes = ctx >= 1

    barrier = pltpu.get_barrier_semaphore()
    for p in range(1, nh):
        greet(barrier, ctx, (head + p) % nh)
    for other in (right, left, across, mate):
        greet(barrier, other, head)
    for side in range(2):
        for step in (JUMP, nz - JUMP):
            greet(barrier, ctx_of(nz, side, (z + step) % nz, core), head)

    @pl.when(takes)
    def _():
        greet(barrier, ctx - 1, last)

    @pl.when(gives)
    def _():
        pl.semaphore_wait(barrier, nh - 1 + 8 + nh)

    @pl.when(jnp.logical_not(gives))
    def _():
        pl.semaphore_wait(barrier, nh - 1 + 8)

    pairs = ((k_in, k_loc), (v_in, v_loc), (q_in, q_out), (cot_in, cot_out))

    def halo_copies():
        out = []
        for a in range(2):
            for t in range(nh):
                out.append(remote(
                    pairs[a][0].at[pl.ds(rows - 16, 16), pl.ds(t * ch, ch)], halo.at[a],
                    h_send.at[a, t], h_recv.at[a], ctx + 1, t))
        return out

    def swaps(a):
        out = []
        for p in range(1, nh):
            t = (head + p) % nh
            out.append(remote(
                pairs[a][0].at[:, col(t, ch)], pairs[a][1].at[col(head, rows), :],
                a_send.at[a, p - 1], a_recv.at[a, p - 1], ctx, t))
        return out

    def own(a):
        return pltpu.make_async_copy(
            pairs[a][0].at[:, col(head, ch)], pairs[a][1].at[col(head, rows), :], a_self.at[a])

    moves = [swaps(a) for a in range(4)]
    for a in range(2):
        own(a).start()
        for m in moves[a]:
            m.start()

    @pl.when(gives)
    def _():
        for m in halo_copies():
            m.start()

    @pl.when(jnp.logical_not(takes))
    def _():
        kf[0:8, :] = jnp.zeros((8, ch), F32)
        vf[0:8, :] = jnp.zeros((8, ch), F32)

    @pl.when(takes)
    def _():
        for a, f in ((0, kf), (1, vf)):
            pltpu.make_async_copy(halo.at[a], halo.at[a], h_recv.at[a]).wait()
            f[0:8, :] = halo[a].astype(F32)[8:16, :]

    count = nh * rows // 4
    for a, f, taps in ((0, kf, kt), (1, vf, vt)):
        own(a).wait()
        for m in moves[a]:
            m.wait_recv()
        f[pl.ds(8, nh * rows), :] = pairs[a][1][...].astype(F32)
        packed = (taps[0:1, :] * f[pl.ds(7, count, stride=4), :]
                  + taps[1:2, :] * f[pl.ds(8, count, stride=4), :]
                  + taps[2:3, :] * f[pl.ds(9, count, stride=4), :])
        kv[core, z, pl.ds(pl.multiple_of(y * count, count), count), a * ch:(a + 1) * ch] = packed.astype(BF16)

    def chunk(zz, u):
        side = y + u - 2 * u * y
        return kv.at[core, zz, pl.ds(pl.multiple_of(side * count, count), count), :]

    def to_mate(zz, u, n):
        return remote(chunk(zz, u), chunk(zz, u), c_send.at[n, u], c_recv.at[n, u], mate, head)

    flows = ((0, 2, 2), (-JUMP, nz // 2 - JUMP, nz // 2 - 1 - JUMP), (JUMP, 2, 2))

    def to_right(f, k, u):
        here = chunk((z + flows[f][0] - k + 2 * nz) % nz, u)
        return remote(here, here, r_send.at[3 * f + k, u], r_recv.at[3 * f + k, u], right, head)

    def to_left(f, k, u):
        here = chunk((z + left_of[f] + k + 2 * nz) % nz, u)
        return remote(here, here, l_send.at[3 * f + k, u], l_recv.at[3 * f + k, u], left, head)

    left_of = (0, JUMP, -JUMP)

    def jump(sign, u):
        side = y + u - 2 * u * y
        here = chunk(z, 0)
        return remote(here, here, j_send.at[sign, u], j_recv.at[sign, u],
                      ctx_of(nz, side, (z + (2 * sign - 1) * JUMP + nz) % nz, core), head)

    step_y = remote(chunk(z, 0), chunk(z, 0), y_send, y_recv, across, head)
    mates = []

    def forward(zz, u, n):
        mates.append(to_mate(zz, u, n))
        mates[-1].start()

    begun = []

    def go(copy):
        copy.start()
        begun.append(copy)

    for sign in range(2):
        go(jump(sign, 0))
    go(to_right(0, 0, 0))
    go(to_left(0, 0, 0))
    step_y.start()
    for sign in range(2):
        go(jump(sign, 1))
    forward(z, 0, 0)
    for a in range(2, 4):
        own(a).start()
        for m in moves[a]:
            m.start()

    def got_right(f, k, u):
        to_right(f, k, u).wait_recv()
        if k + 1 < flows[f][1]:
            go(to_right(f, k + 1, u))
        forward((z - 1 + flows[f][0] - k + 2 * nz) % nz, u, 1 + 3 * f + k)

    def got_left(f, k, u):
        to_left(f, k, u).wait_recv()
        if k + 1 < flows[f][2]:
            go(to_left(f, k + 1, u))
        forward((z + 1 + left_of[f] + k + 2 * nz) % nz, u, 10 + 3 * f + k)

    got_right(0, 0, 0)
    got_left(0, 0, 0)
    step_y.wait_recv()
    go(to_right(0, 0, 1))
    go(to_left(0, 0, 1))
    forward(z, 1, 0)
    for u in range(2):
        for sign in (1, 0):
            jump(sign, u).wait_recv()
            if sign == 1:
                go(to_right(1, 0, u))
                go(to_left(2, 0, u))
            else:
                go(to_right(2, 0, u))
                go(to_left(1, 0, u))
            forward((z - (2 * sign - 1) * JUMP + nz) % nz, u, 19 + sign)
    got_right(0, 1, 0)
    got_left(0, 1, 0)
    got_right(0, 0, 1)
    got_left(0, 0, 1)
    for k in range(3):
        for u in range(2):
            for f in (1, 2):
                if k < flows[f][1]:
                    got_right(f, k, u)
                if k < flows[f][2]:
                    got_left(f, k, u)
        if k == 0:
            got_right(0, 1, 1)
            got_left(0, 1, 1)
    for a in range(2, 4):
        own(a).wait()
        for m in moves[a]:
            m.wait_recv()
    for m in mates:
        m.wait()
    for m in begun:
        m.wait_send()
    step_y.wait_send()
    for a in range(4):
        for m in moves[a]:
            m.wait_send()

    @pl.when(gives)
    def _():
        for m in halo_copies():
            m.wait_send()


def gather(nz, nh, q, k, v, cot, kt, vt):
    rows, width = q.shape
    ch = width // nh
    length = nh * rows
    count = length // 4
    vm = pl.BlockSpec(memory_space=pltpu.VMEM)
    dma = pltpu.SemaphoreType.DMA
    return pl.pallas_call(
        functools.partial(gather_kernel, nz, nh),
        out_shape=(
            jax.ShapeDtypeStruct((length, ch), BF16),
            jax.ShapeDtypeStruct((length, ch), BF16),
            jax.ShapeDtypeStruct((length + 8, ch), F32),
            jax.ShapeDtypeStruct((length + 8, ch), F32),
            jax.ShapeDtypeStruct((2, nz, 2 * count, 2 * ch), BF16),
        ),
        in_specs=[pl.BlockSpec(memory_space=pltpu.HBM)] * 4 + [vm] * 2,
        out_specs=(vm,) * 5,
        scratch_shapes=[
            pltpu.VMEM((length, ch), BF16),
            pltpu.VMEM((length, ch), BF16),
            pltpu.VMEM((2, 16, ch), BF16),
            dma((4, nh - 1)), dma((4, nh - 1)), dma((4,)),
            dma((2, nh)), dma((2,)),
            dma(()), dma(()),
            dma((9, 2)), dma((9, 2)),
            dma((9, 2)), dma((9, 2)),
            dma((21, 2)), dma((21, 2)),
            dma((2, 2)), dma((2, 2)),
        ],
        compiler_params=pltpu.CompilerParams(
            collective_id=0, has_side_effects=True, vmem_limit_bytes=40 << 20),
        name="gather",
    )(q, k, v, cot, kt, vt)


def scatter_kernel(nz, nh, part, att_in, gq_in, kf, vf, kt, vt,
                   att_out, gq_out, gk_out, gv_out, kt_out, vt_out,
                   pin, rbuf, rout, lbuf, lout, jbuf, jout, ybuf, yout, spread, gk_loc, gv_loc,
                   edge, edge_in, tap1, tap2,
                   a_send, a_recv, a_self, e_send, e_recv,
                   y_send, y_recv, r_send, r_recv, l_send, l_recv, c_send, c_recv,
                   t_send, t_recv, u_send, u_recv, j_send, j_recv):
    ctx, head, y, z, core = place(nz)
    nctx = 4 * nz
    rows = att_out.shape[0]
    ch = att_in.shape[1]
    count = nh * rows // 4
    zr, zl = (z + 1) % nz, (z + nz - 1) % nz
    right, left = ctx_of(nz, y, zr, core), ctx_of(nz, y, zl, core)
    across = ctx_of(nz, 1 - y, z, core)
    mate = ctx_of(nz, y, z, 1 - core)
    corner = ctx_of(nz, 1 - y, z, 1 - core)
    last = nh - 1
    takes = (head == last) & (ctx < nctx - 1)
    gives = ctx >= 1

    barrier = pltpu.get_barrier_semaphore()
    for p in range(1, nh):
        greet(barrier, ctx, (head + p) % nh)
    for p in range(1, nz):
        greet(barrier, ctx_of(nz, y, (z + p) % nz, core), head)
    for other in (across, mate, corner):
        greet(barrier, other, head)

    @pl.when(takes)
    def _():
        for t in range(nh):
            greet(barrier, ctx + 1, t)

    @pl.when(gives)
    def _():
        pl.semaphore_wait(barrier, nh - 1 + nz - 1 + 3 + 1)

    @pl.when(jnp.logical_not(gives))
    def _():
        pl.semaphore_wait(barrier, nh - 1 + nz - 1 + 3)


    def to_mate(zz, n):
        return remote(part.at[1 - core, zz], pin.at[zz], c_send.at[n], c_recv.at[n], mate, head)

    offsets = (-8, 7, 3, -3, -7, 6, 4, -4, -6, -5, 5, -2, 2, -1, 1, 0)
    order = [(z + o + 2 * nz) % nz for o in offsets]
    mates = [to_mate(zz, n) for n, zz in enumerate(order)]
    for m in mates:
        m.start()

    pairs = ((att_in, att_out), (gq_in, gq_out), (gk_loc, gk_out), (gv_loc, gv_out))

    def swaps(a):
        out = []
        for p in range(1, nh):
            t = (head + p) % nh
            out.append(remote(
                pairs[a][0].at[col(t, rows), :], pairs[a][1].at[:, col(head, ch)],
                a_send.at[a, p - 1], a_recv.at[a, p - 1], ctx, t))
        return out

    def own(a):
        return pltpu.make_async_copy(
            pairs[a][0].at[col(head, rows), :], pairs[a][1].at[:, col(head, ch)], a_self.at[a])

    moves = [swaps(a) for a in range(4)]
    for a in range(2):
        own(a).start()
        for m in moves[a]:
            m.start()

    def part_of(u):
        side = 1 - y - u + 2 * u * y
        return pl.ds(pl.multiple_of(side * count, count), count)

    def local_sum(o, u):
        n = offsets.index(o)
        if u == 0:
            mates[n].wait_recv()
        zz = order[n]
        return part[core, zz, part_of(u), :].astype(F32) + pin[zz, part_of(u), :].astype(F32)

    lefts = ((-8, -7, -6), (3, 4), (-2, -1))
    rights = ((7, 6), (-3, -4), (2, 1))

    def to_right(f, k, u):
        return remote(rout.at[3 * f + k, u], rbuf.at[3 * f + k, u],
                      r_send.at[3 * f + k, u], r_recv.at[3 * f + k, u], right, head)

    def to_left(f, k, u):
        return remote(lout.at[3 * f + k, u], lbuf.at[3 * f + k, u],
                      l_send.at[3 * f + k, u], l_recv.at[3 * f + k, u], left, head)

    def jump(sign, u):
        return remote(jout.at[sign, u], jbuf.at[sign, u], j_send.at[sign, u], j_recv.at[sign, u],
                      ctx_of(nz, y, (z + (2 * sign - 1) * JUMP + nz) % nz, core), head)

    begun = []

    def from_left(f, k, u):
        to_right(f, k, u).wait_recv()
        return rbuf[3 * f + k, u].astype(F32)

    def from_right(f, k, u):
        to_left(f, k, u).wait_recv()
        return lbuf[3 * f + k, u].astype(F32)

    def push_right(f, k, u):
        total = local_sum(rights[f][k], u)
        if k > 0:
            total = total + from_left(f, k - 1, u)
        rout[3 * f + k, u] = total.astype(BF16)
        begun.append(to_right(f, k, u))
        begun[-1].start()

    def push_left(f, k, u):
        total = local_sum(lefts[f][k], u)
        if k > 0:
            total = total + from_right(f, k - 1, u)
        lout[3 * f + k, u] = total.astype(BF16)
        begun.append(to_left(f, k, u))
        begun[-1].start()

    def push_jump(sign, total, u):
        jout[sign, u] = total.astype(BF16)
        begun.append(jump(sign, u))
        begun[-1].start()

    for k in range(2):
        for u in range(2):
            push_left(0, k, u)
            push_right(0, k, u)
            push_left(1, k, u)
            push_right(1, k, u)
    for u in range(2):
        push_left(0, 2, u)
    for u in range(2):
        push_left(2, 0, u)
        push_right(2, 0, u)
    for u in range(2):
        push_jump(1, local_sum(5, u) + from_left(0, 1, u) + from_right(1, 1, u), u)
    for u in range(2):
        push_left(2, 1, u)
        push_right(2, 1, u)
        push_jump(0, local_sum(-5, u) + from_right(0, 2, u) + from_left(1, 1, u), u)
    for u in range(2):
        total = local_sum(0, u) + from_right(2, 1, u) + from_left(2, 1, u)
        for sign in range(2):
            jump(sign, u).wait_recv()
            total = total + jbuf[sign, u].astype(F32)
        if u == 0:
            ybuf[...] = total.astype(BF16)
            step_y = remote(ybuf, yout, y_send, y_recv, across, head)
            step_y.start()
        else:
            step_y.wait_recv()
            grads = total + yout[...].astype(F32)

    tap1[z, 6:8, :] = jnp.zeros((2, ch), F32)
    for a, f, taps, loc in ((0, kf, kt, gk_loc), (1, vf, vt, gv_loc)):
        g = grads[:, a * ch:(a + 1) * ch]
        spread[a, 0:8, :] = jnp.zeros((8, ch), F32)
        spread[a, pl.ds(nh * rows, 8), :] = jnp.zeros((8, ch), F32)
        spread[a, pl.ds(7, count, stride=4), :] = taps[0:1, :] * g
        spread[a, pl.ds(8, count, stride=4), :] = taps[1:2, :] * g
        spread[a, pl.ds(9, count, stride=4), :] = taps[2:3, :] * g
        spread[a, pl.ds(10, count, stride=4), :] = jnp.zeros((count, ch), F32)
        spread[a, pl.ds(nh * rows + 7, 1), :] = jnp.zeros((1, ch), F32)
        loc[...] = spread[a, pl.ds(8, nh * rows), :].astype(BF16)
        edge[a] = jnp.concatenate([jnp.zeros((8, ch), F32), spread[a, 0:8, :]], axis=0).astype(BF16)
        for t in range(3):
            tap1[z, 3 * a + t:3 * a + t + 1, :] = jnp.sum(
                g * f[pl.ds(7 + t, count, stride=4), :], axis=0, keepdims=True)

    def tap_z():
        out = []
        for p in range(1, nz):
            out.append(remote(tap1.at[z], tap1.at[z], t_send.at[p - 1], t_recv.at[p - 1],
                              ctx_of(nz, y, (z + p) % nz, core), head))
        return out

    def tap_yc():
        out = []
        for m, other in enumerate((across, mate, corner)):
            spot = tap2.at[2 * y + core]
            out.append(remote(spot, spot, u_send.at[m], u_recv.at[m], other, head))
        return out

    def edges():
        return [remote(edge.at[a], edge_in.at[a, head], e_send.at[a], e_recv.at[a, head],
                       ctx - 1, last) for a in range(2)]

    for m in tap_z():
        m.start()

    @pl.when(gives)
    def _():
        for m in edges():
            m.start()

    for a in range(2, 4):
        own(a).start()
        for m in moves[a]:
            m.start()

    for m in tap_z():
        m.wait_recv()
    total = tap1[0]
    for i in range(1, nz):
        total = total + tap1[i]
    tap2[2 * y + core] = total
    for m in tap_yc():
        m.start()

    for a in range(4):
        own(a).wait()
        for m in moves[a]:
            m.wait_recv()

    @pl.when(takes)
    def _():
        for a in range(2):
            for t in range(nh):
                pltpu.make_async_copy(edge_in.at[a, t], edge_in.at[a, t], e_recv.at[a, t]).wait()
                spot = (pl.ds(rows - 16, 16), pl.ds(t * ch, ch))
                out = pairs[2 + a][1]
                out[spot] = (out[spot].astype(F32) + edge_in[a, t].astype(F32)).astype(BF16)

    for m in tap_yc():
        m.wait_recv()
    total = (tap2[0] + tap2[1]) + (tap2[2] + tap2[3])
    kt_out[...] = total[0:3, :]
    vt_out[...] = total[3:6, :]

    for m in mates:
        m.wait_send()
    for m in begun:
        m.wait_send()
    step_y.wait_send()
    for a in range(4):
        for m in moves[a]:
            m.wait_send()
    for m in tap_z():
        m.wait_send()
    for m in tap_yc():
        m.wait_send()

    @pl.when(gives)
    def _():
        for m in edges():
            m.wait_send()


def scatter(nz, nh, part, att, gq, kf, vf, kt, vt):
    length, ch = att.shape
    rows = length // nh
    count = length // 4
    vm = pl.BlockSpec(memory_space=pltpu.VMEM)
    dma = pltpu.SemaphoreType.DMA
    wide = jax.ShapeDtypeStruct((rows, nh * ch), BF16)
    small = jax.ShapeDtypeStruct((3, ch), F32)
    return pl.pallas_call(
        functools.partial(scatter_kernel, nz, nh),
        out_shape=(wide, wide, wide, wide, small, small),
        in_specs=[vm] * 7,
        out_specs=(vm,) * 6,
        scratch_shapes=[
            pltpu.VMEM((nz, 2 * count, 2 * ch), BF16),
            pltpu.VMEM((9, 2, count, 2 * ch), BF16),
            pltpu.VMEM((9, 2, count, 2 * ch), BF16),
            pltpu.VMEM((9, 2, count, 2 * ch), BF16),
            pltpu.VMEM((9, 2, count, 2 * ch), BF16),
            pltpu.VMEM((2, 2, count, 2 * ch), BF16),
            pltpu.VMEM((2, 2, count, 2 * ch), BF16),
            pltpu.VMEM((count, 2 * ch), BF16),
            pltpu.VMEM((count, 2 * ch), BF16),
            pltpu.VMEM((2, length + 16, ch), F32),
            pltpu.VMEM((length, ch), BF16),
            pltpu.VMEM((length, ch), BF16),
            pltpu.VMEM((2, 16, ch), BF16),
            pltpu.VMEM((2, nh, 16, ch), BF16),
            pltpu.VMEM((nz, 8, ch), F32),
            pltpu.VMEM((4, 8, ch), F32),
            dma((4, nh - 1)), dma((4, nh - 1)), dma((4,)),
            dma((2,)), dma((2, nh)),
            dma(()), dma(()),
            dma((9, 2)), dma((9, 2)),
            dma((9, 2)), dma((9, 2)),
            dma((nz,)), dma((nz,)),
            dma((nz - 1,)), dma((nz - 1,)),
            dma((3,)), dma((3,)),
            dma((2, 2)), dma((2, 2)),
        ],
        compiler_params=pltpu.CompilerParams(
            collective_id=1, has_side_effects=True, vmem_limit_bytes=40 << 20),
        name="scatter",
    )(part, att, gq, kf, vf, kt, vt)


def attention_kernel(block, q_ref, cot_ref, kv_ref, att_ref, gq_ref, part_ref,
                     s_ref, e_ref, att_t, gq_t):
    length, ch = q_ref.shape
    half = ch // 2
    keys = kv_ref.shape[0]
    steps = keys // block
    scaling = half ** (-0.5)
    lanes = lax.broadcasted_iota(jnp.int32, (length, ch), 1)

    def split(x):
        x = x.astype(F32)
        zero = jnp.zeros_like(x)
        return jnp.concatenate(
            [jnp.where(lanes < half, x, zero), jnp.where(lanes < half, zero, x)], axis=0).astype(BF16)

    def dot(a, b, ca, cb):
        return lax.dot_general(a, b, (((ca,), (cb,)), ((), ())), preferred_element_type=F32)

    qs = split(q_ref[...].astype(F32) * scaling)
    cots = split(cot_ref[...])

    def at(i):
        return pl.ds(pl.multiple_of(i * block, block), block)

    def scores(i, top):
        s = dot(kv_ref[at(i), 0:ch], qs, 1, 1)
        s_ref[at(i), :] = s
        return jnp.maximum(top, jnp.max(s.reshape(block // 8, 8, 2 * length), axis=0))

    top = lax.fori_loop(0, steps, scores, jnp.full((8, 2 * length), -jnp.inf, F32))
    top = jnp.max(top, axis=0, keepdims=True)

    att_t[...] = jnp.zeros_like(att_t)
    gq_t[...] = jnp.zeros_like(gq_t)

    def raise_(i, total):
        e = jnp.exp(s_ref[at(i), :] - top)
        eb = e.astype(BF16)
        e_ref[at(i), :] = eb
        att_t[...] += dot(kv_ref[at(i), ch:2 * ch], eb, 0, 0)
        return total + jnp.sum(e.reshape(block // 8, 8, 2 * length), axis=0)

    total = lax.fori_loop(0, steps, raise_, jnp.zeros((8, 2 * length), F32))
    inv = 1.0 / jnp.sum(total, axis=0, keepdims=True)

    def join(x):
        return jnp.concatenate([x[0:half, 0:length], x[half:ch, length:2 * length]], axis=0)

    att = jnp.transpose(join(att_t[...] * inv)).astype(BF16)
    att_ref[...] = att
    prod = jnp.transpose(cot_ref[...].astype(F32) * att.astype(F32))
    offset = jnp.concatenate(
        [jnp.sum(prod[0:half], axis=0, keepdims=True),
         jnp.sum(prod[half:ch], axis=0, keepdims=True)], axis=1)

    def back(i, carry):
        w = e_ref[at(i), :].astype(F32) * inv
        dw = dot(kv_ref[at(i), ch:2 * ch], cots, 1, 1)
        ds = (w * (dw - offset)).astype(BF16)
        part_ref[at(i), 0:ch] = dot(ds, qs, 1, 0).astype(BF16)
        part_ref[at(i), ch:2 * ch] = dot(w.astype(BF16), cots, 1, 0).astype(BF16)
        gq_t[...] += dot(kv_ref[at(i), 0:ch], ds, 0, 0)
        return carry

    lax.fori_loop(0, steps, back, 0)
    gq_ref[...] = (jnp.transpose(join(gq_t[...])) * scaling).astype(BF16)


def attention(q, cot, kv):
    length, ch = q.shape
    flat = kv.reshape(-1, 2 * ch)
    keys = flat.shape[0]
    vm = pl.BlockSpec(memory_space=pltpu.VMEM)
    att, gq, part = pl.pallas_call(
        functools.partial(attention_kernel, 512),
        out_shape=(
            jax.ShapeDtypeStruct((length, ch), BF16),
            jax.ShapeDtypeStruct((length, ch), BF16),
            jax.ShapeDtypeStruct((keys, 2 * ch), BF16),
        ),
        in_specs=[vm] * 3,
        out_specs=(vm,) * 3,
        scratch_shapes=[
            pltpu.VMEM((keys, 2 * length), F32),
            pltpu.VMEM((keys, 2 * length), BF16),
            pltpu.VMEM((ch, 2 * length), F32),
            pltpu.VMEM((ch, 2 * length), F32),
        ],
        compiler_params=pltpu.CompilerParams(vmem_limit_bytes=48 << 20),
        name="attention",
    )(q, cot, flat)
    return att, gq, part.reshape(kv.shape)


def local(query_rows, key_rows, value_rows, cotangent, key_taps, value_taps):
    nz = lax.axis_size("ctx") // 4
    nh = lax.axis_size("head")
    q, cot, kf, vf, kv = gather(
        nz, nh, query_rows, key_rows, value_rows, cotangent, key_taps, value_taps)
    att, gq, part = attention(q, cot, kv)
    return scatter(nz, nh, part, att, gq, kf, vf, key_taps, value_taps)


def solution(mesh):
    rows = P(("ctx", "head"), None)
    taps = P(None, "head")
    return jax.shard_map(
        local,
        mesh=mesh,
        in_specs=(rows, rows, rows, rows, taps, taps),
        out_specs=(rows, rows, rows, rows, taps, taps),
        check_vma=False,
    )
```

```python
import functools

import jax
import jax.numpy as jnp
from jax import lax
from jax.experimental import pallas as pl
from jax.experimental.pallas import tpu as pltpu
from jax.sharding import PartitionSpec as P

MESH = pl.DeviceIdType.MESH
F32 = jnp.float32
JUMP = 5
BF16 = jnp.bfloat16


def place(nz):
    ctx = lax.axis_index("ctx")
    head = lax.axis_index("head")
    core = ctx % 2
    z = (ctx // 2) % nz
    y = ctx // (2 * nz)
    return ctx, head, y, z, core


def ctx_of(nz, y, z, core):
    return (y * nz + z) * 2 + core


def remote(src, dst, send, recv, ctx, head):
    return pltpu.make_async_remote_copy(
        src_ref=src, dst_ref=dst, send_sem=send, recv_sem=recv,
        device_id={"ctx": ctx, "head": head}, device_id_type=MESH,
    )


def greet(sem, ctx, head):
    pl.semaphore_signal(sem, inc=1, device_id={"ctx": ctx, "head": head}, device_id_type=MESH)


def col(h, width):
    return pl.ds(pl.multiple_of(h * width, width), width)


def gather_kernel(nz, nh, q_in, k_in, v_in, cot_in, kt, vt,
                  q_out, cot_out, kf, vf, kv,
                  k_loc, v_loc, halo,
                  a_send, a_recv, a_self, h_send, h_recv,
                  y_send, y_recv, r_send, r_recv, l_send, l_recv, c_send, c_recv, j_send, j_recv):
    ctx, head, y, z, core = place(nz)
    nctx = 4 * nz
    rows = q_in.shape[0]
    ch = q_out.shape[1]
    zr, zl = (z + 1) % nz, (z + nz - 1) % nz
    right, left = ctx_of(nz, y, zr, core), ctx_of(nz, y, zl, core)
    across = ctx_of(nz, 1 - y, z, core)
    mate = ctx_of(nz, y, z, 1 - core)
    last = nh - 1
    gives = (head == last) & (ctx < nctx - 1)
    takes = ctx >= 1

    barrier = pltpu.get_barrier_semaphore()
    for p in range(1, nh):
        greet(barrier, ctx, (head + p) % nh)
    for other in (right, left, across, mate):
        greet(barrier, other, head)
    for side in range(2):
        for step in (JUMP, nz - JUMP):
            greet(barrier, ctx_of(nz, side, (z + step) % nz, core), head)

    @pl.when(takes)
    def _():
        greet(barrier, ctx - 1, last)

    @pl.when(gives)
    def _():
        pl.semaphore_wait(barrier, nh - 1 + 8 + nh)

    @pl.when(jnp.logical_not(gives))
    def _():
        pl.semaphore_wait(barrier, nh - 1 + 8)

    pairs = ((k_in, k_loc), (v_in, v_loc), (q_in, q_out), (cot_in, cot_out))

    def halo_copies():
        out = []
        for a in range(2):
            for t in range(nh):
                out.append(remote(
                    pairs[a][0].at[pl.ds(rows - 16, 16), pl.ds(t * ch, ch)], halo.at[a],
                    h_send.at[a, t], h_recv.at[a], ctx + 1, t))
        return out

    def swaps(a):
        out = []
        for p in range(1, nh):
            t = (head + p) % nh
            out.append(remote(
                pairs[a][0].at[:, col(t, ch)], pairs[a][1].at[col(head, rows), :],
                a_send.at[a, p - 1], a_recv.at[a, p - 1], ctx, t))
        return out

    def own(a):
        return pltpu.make_async_copy(
            pairs[a][0].at[:, col(head, ch)], pairs[a][1].at[col(head, rows), :], a_self.at[a])

    moves = [swaps(a) for a in range(4)]
    for a in range(2):
        own(a).start()
        for m in moves[a]:
            m.start()

    @pl.when(gives)
    def _():
        for m in halo_copies():
            m.start()

    for a in range(2, 4):
        own(a).start()
        for m in moves[a]:
            m.start()

    @pl.when(jnp.logical_not(takes))
    def _():
        kf[0:8, :] = jnp.zeros((8, ch), F32)
        vf[0:8, :] = jnp.zeros((8, ch), F32)

    @pl.when(takes)
    def _():
        for a, f in ((0, kf), (1, vf)):
            pltpu.make_async_copy(halo.at[a], halo.at[a], h_recv.at[a]).wait()
            f[0:8, :] = halo[a].astype(F32)[8:16, :]

    count = nh * rows // 4
    for a, f, taps in ((0, kf, kt), (1, vf, vt)):
        own(a).wait()
        for m in moves[a]:
            m.wait_recv()
        f[pl.ds(8, nh * rows), :] = pairs[a][1][...].astype(F32)
        packed = (taps[0:1, :] * f[pl.ds(7, count, stride=4), :]
                  + taps[1:2, :] * f[pl.ds(8, count, stride=4), :]
                  + taps[2:3, :] * f[pl.ds(9, count, stride=4), :])
        kv[core, z, pl.ds(pl.multiple_of(y * count, count), count), a * ch:(a + 1) * ch] = packed.astype(BF16)

    def chunk(zz, u):
        side = y + u - 2 * u * y
        return kv.at[core, zz, pl.ds(pl.multiple_of(side * count, count), count), :]

    def to_mate(zz, u, n):
        return remote(chunk(zz, u), chunk(zz, u), c_send.at[n, u], c_recv.at[n, u], mate, head)

    flows = ((0, 2, 2), (-JUMP, nz // 2 - JUMP, nz // 2 - 1 - JUMP), (JUMP, 2, 2))

    def to_right(f, k, u):
        here = chunk((z + flows[f][0] - k + 2 * nz) % nz, u)
        return remote(here, here, r_send.at[3 * f + k, u], r_recv.at[3 * f + k, u], right, head)

    def to_left(f, k, u):
        here = chunk((z + left_of[f] + k + 2 * nz) % nz, u)
        return remote(here, here, l_send.at[3 * f + k, u], l_recv.at[3 * f + k, u], left, head)

    left_of = (0, JUMP, -JUMP)

    def jump(sign, u):
        side = y + u - 2 * u * y
        here = chunk(z, 0)
        return remote(here, here, j_send.at[sign, u], j_recv.at[sign, u],
                      ctx_of(nz, side, (z + (2 * sign - 1) * JUMP + nz) % nz, core), head)

    step_y = remote(chunk(z, 0), chunk(z, 0), y_send, y_recv, across, head)
    mates = []

    def forward(zz, u, n):
        mates.append(to_mate(zz, u, n))
        mates[-1].start()

    begun = []

    def go(copy):
        copy.start()
        begun.append(copy)

    for sign in range(2):
        go(jump(sign, 0))
    go(to_right(0, 0, 0))
    go(to_left(0, 0, 0))
    step_y.start()
    for sign in range(2):
        go(jump(sign, 1))
    forward(z, 0, 0)

    def got_right(f, k, u):
        to_right(f, k, u).wait_recv()
        if k + 1 < flows[f][1]:
            go(to_right(f, k + 1, u))
        forward((z - 1 + flows[f][0] - k + 2 * nz) % nz, u, 1 + 3 * f + k)

    def got_left(f, k, u):
        to_left(f, k, u).wait_recv()
        if k + 1 < flows[f][2]:
            go(to_left(f, k + 1, u))
        forward((z + 1 + left_of[f] + k + 2 * nz) % nz, u, 10 + 3 * f + k)

    got_right(0, 0, 0)
    got_left(0, 0, 0)
    step_y.wait_recv()
    go(to_right(0, 0, 1))
    go(to_left(0, 0, 1))
    forward(z, 1, 0)
    for u in range(2):
        for sign in (1, 0):
            jump(sign, u).wait_recv()
            if sign == 1:
                go(to_right(1, 0, u))
                go(to_left(2, 0, u))
            else:
                go(to_right(2, 0, u))
                go(to_left(1, 0, u))
            forward((z - (2 * sign - 1) * JUMP + nz) % nz, u, 19 + sign)
    got_right(0, 1, 0)
    got_left(0, 1, 0)
    got_right(0, 0, 1)
    got_left(0, 0, 1)
    for k in range(3):
        for u in range(2):
            for f in (1, 2):
                if k < flows[f][1]:
                    got_right(f, k, u)
                if k < flows[f][2]:
                    got_left(f, k, u)
        if k == 0:
            got_right(0, 1, 1)
            got_left(0, 1, 1)
    for a in range(2, 4):
        own(a).wait()
        for m in moves[a]:
            m.wait_recv()
    for m in mates:
        m.wait()
    for m in begun:
        m.wait_send()
    step_y.wait_send()
    for a in range(4):
        for m in moves[a]:
            m.wait_send()

    @pl.when(gives)
    def _():
        for m in halo_copies():
            m.wait_send()


def gather(nz, nh, q, k, v, cot, kt, vt):
    rows, width = q.shape
    ch = width // nh
    length = nh * rows
    count = length // 4
    vm = pl.BlockSpec(memory_space=pltpu.VMEM)
    dma = pltpu.SemaphoreType.DMA
    return pl.pallas_call(
        functools.partial(gather_kernel, nz, nh),
        out_shape=(
            jax.ShapeDtypeStruct((length, ch), BF16),
            jax.ShapeDtypeStruct((length, ch), BF16),
            jax.ShapeDtypeStruct((length + 8, ch), F32),
            jax.ShapeDtypeStruct((length + 8, ch), F32),
            jax.ShapeDtypeStruct((2, nz, 2 * count, 2 * ch), BF16),
        ),
        in_specs=[pl.BlockSpec(memory_space=pltpu.HBM)] * 4 + [vm] * 2,
        out_specs=(vm,) * 5,
        scratch_shapes=[
            pltpu.VMEM((length, ch), BF16),
            pltpu.VMEM((length, ch), BF16),
            pltpu.VMEM((2, 16, ch), BF16),
            dma((4, nh - 1)), dma((4, nh - 1)), dma((4,)),
            dma((2, nh)), dma((2,)),
            dma(()), dma(()),
            dma((9, 2)), dma((9, 2)),
            dma((9, 2)), dma((9, 2)),
            dma((21, 2)), dma((21, 2)),
            dma((2, 2)), dma((2, 2)),
        ],
        compiler_params=pltpu.CompilerParams(
            collective_id=0, has_side_effects=True, vmem_limit_bytes=40 << 20),
        name="gather",
    )(q, k, v, cot, kt, vt)


def scatter_kernel(nz, nh, part, att_in, gq_in, kf, vf, kt, vt,
                   att_out, gq_out, gk_out, gv_out, kt_out, vt_out,
                   pin, rbuf, rout, lbuf, lout, jbuf, jout, ybuf, yout, spread, gk_loc, gv_loc,
                   edge, edge_in, tap1, tap2,
                   a_send, a_recv, a_self, e_send, e_recv,
                   y_send, y_recv, r_send, r_recv, l_send, l_recv, c_send, c_recv,
                   t_send, t_recv, u_send, u_recv, j_send, j_recv):
    ctx, head, y, z, core = place(nz)
    nctx = 4 * nz
    rows = att_out.shape[0]
    ch = att_in.shape[1]
    count = nh * rows // 4
    zr, zl = (z + 1) % nz, (z + nz - 1) % nz
    right, left = ctx_of(nz, y, zr, core), ctx_of(nz, y, zl, core)
    across = ctx_of(nz, 1 - y, z, core)
    mate = ctx_of(nz, y, z, 1 - core)
    corner = ctx_of(nz, 1 - y, z, 1 - core)
    last = nh - 1
    takes = (head == last) & (ctx < nctx - 1)
    gives = ctx >= 1

    barrier = pltpu.get_barrier_semaphore()
    for p in range(1, nh):
        greet(barrier, ctx, (head + p) % nh)
    for p in range(1, nz):
        greet(barrier, ctx_of(nz, y, (z + p) % nz, core), head)
    for other in (across, mate, corner):
        greet(barrier, other, head)

    @pl.when(takes)
    def _():
        for t in range(nh):
            greet(barrier, ctx + 1, t)

    @pl.when(gives)
    def _():
        pl.semaphore_wait(barrier, nh - 1 + nz - 1 + 3 + 1)

    @pl.when(jnp.logical_not(gives))
    def _():
        pl.semaphore_wait(barrier, nh - 1 + nz - 1 + 3)


    def to_mate(zz, n):
        return remote(part.at[1 - core, zz], pin.at[zz], c_send.at[n], c_recv.at[n], mate, head)

    offsets = (-8, 7, 3, -3, -7, 6, 4, -4, -6, -5, 5, -2, 2, -1, 1, 0)
    order = [(z + o + 2 * nz) % nz for o in offsets]
    mates = [to_mate(zz, n) for n, zz in enumerate(order)]
    for m in mates:
        m.start()

    pairs = ((att_in, att_out), (gq_in, gq_out), (gk_loc, gk_out), (gv_loc, gv_out))

    def swaps(a):
        out = []
        for p in range(1, nh):
            t = (head + p) % nh
            out.append(remote(
                pairs[a][0].at[col(t, rows), :], pairs[a][1].at[:, col(head, ch)],
                a_send.at[a, p - 1], a_recv.at[a, p - 1], ctx, t))
        return out

    def own(a):
        return pltpu.make_async_copy(
            pairs[a][0].at[col(head, rows), :], pairs[a][1].at[:, col(head, ch)], a_self.at[a])

    moves = [swaps(a) for a in range(4)]
    def part_of(u):
        side = 1 - y - u + 2 * u * y
        return pl.ds(pl.multiple_of(side * count, count), count)

    def local_sum(o, u):
        n = offsets.index(o)
        if u == 0:
            mates[n].wait_recv()
        zz = order[n]
        return part[core, zz, part_of(u), :].astype(F32) + pin[zz, part_of(u), :].astype(F32)

    lefts = ((-8, -7, -6), (3, 4), (-2, -1))
    rights = ((7, 6), (-3, -4), (2, 1))

    def to_right(f, k, u):
        return remote(rout.at[3 * f + k, u], rbuf.at[3 * f + k, u],
                      r_send.at[3 * f + k, u], r_recv.at[3 * f + k, u], right, head)

    def to_left(f, k, u):
        return remote(lout.at[3 * f + k, u], lbuf.at[3 * f + k, u],
                      l_send.at[3 * f + k, u], l_recv.at[3 * f + k, u], left, head)

    def jump(sign, u):
        return remote(jout.at[sign, u], jbuf.at[sign, u], j_send.at[sign, u], j_recv.at[sign, u],
                      ctx_of(nz, y, (z + (2 * sign - 1) * JUMP + nz) % nz, core), head)

    begun = []

    def from_left(f, k, u):
        to_right(f, k, u).wait_recv()
        return rbuf[3 * f + k, u].astype(F32)

    def from_right(f, k, u):
        to_left(f, k, u).wait_recv()
        return lbuf[3 * f + k, u].astype(F32)

    def push_right(f, k, u):
        total = local_sum(rights[f][k], u)
        if k > 0:
            total = total + from_left(f, k - 1, u)
        rout[3 * f + k, u] = total.astype(BF16)
        begun.append(to_right(f, k, u))
        begun[-1].start()

    def push_left(f, k, u):
        total = local_sum(lefts[f][k], u)
        if k > 0:
            total = total + from_right(f, k - 1, u)
        lout[3 * f + k, u] = total.astype(BF16)
        begun.append(to_left(f, k, u))
        begun[-1].start()

    def push_jump(sign, total, u):
        jout[sign, u] = total.astype(BF16)
        begun.append(jump(sign, u))
        begun[-1].start()

    for k in range(2):
        for u in range(2):
            push_left(0, k, u)
            push_right(0, k, u)
            push_left(1, k, u)
            push_right(1, k, u)
        if k == 0:
            for a in range(2):
                own(a).start()
                for m in moves[a]:
                    m.start()
    for u in range(2):
        push_left(0, 2, u)
    for u in range(2):
        push_left(2, 0, u)
        push_right(2, 0, u)
    for u in range(2):
        push_jump(1, local_sum(5, u) + from_left(0, 1, u) + from_right(1, 1, u), u)
    for u in range(2):
        push_left(2, 1, u)
        push_right(2, 1, u)
        push_jump(0, local_sum(-5, u) + from_right(0, 2, u) + from_left(1, 1, u), u)
    for u in range(2):
        total = local_sum(0, u) + from_right(2, 1, u) + from_left(2, 1, u)
        for sign in range(2):
            jump(sign, u).wait_recv()
            total = total + jbuf[sign, u].astype(F32)
        if u == 0:
            ybuf[...] = total.astype(BF16)
            step_y = remote(ybuf, yout, y_send, y_recv, across, head)
            step_y.start()
        else:
            step_y.wait_recv()
            grads = total + yout[...].astype(F32)

    tap1[z, 6:8, :] = jnp.zeros((2, ch), F32)
    for a, f in ((0, kf), (1, vf)):
        g = grads[:, a * ch:(a + 1) * ch]
        for t in range(3):
            tap1[z, 3 * a + t:3 * a + t + 1, :] = jnp.sum(
                g * f[pl.ds(7 + t, count, stride=4), :], axis=0, keepdims=True)

    def tap_z():
        out = []
        for p in range(1, nz):
            out.append(remote(tap1.at[z], tap1.at[z], t_send.at[p - 1], t_recv.at[p - 1],
                              ctx_of(nz, y, (z + p) % nz, core), head))
        return out

    for m in tap_z():
        m.start()

    for a, taps, loc in ((0, kt, gk_loc), (1, vt, gv_loc)):
        g = grads[:, a * ch:(a + 1) * ch]
        spread[a, 0:8, :] = jnp.zeros((8, ch), F32)
        spread[a, pl.ds(nh * rows, 8), :] = jnp.zeros((8, ch), F32)
        spread[a, pl.ds(7, count, stride=4), :] = taps[0:1, :] * g
        spread[a, pl.ds(8, count, stride=4), :] = taps[1:2, :] * g
        spread[a, pl.ds(9, count, stride=4), :] = taps[2:3, :] * g
        spread[a, pl.ds(10, count, stride=4), :] = jnp.zeros((count, ch), F32)
        spread[a, pl.ds(nh * rows + 7, 1), :] = jnp.zeros((1, ch), F32)
        loc[...] = spread[a, pl.ds(8, nh * rows), :].astype(BF16)
        edge[a] = jnp.concatenate([jnp.zeros((8, ch), F32), spread[a, 0:8, :]], axis=0).astype(BF16)

    def tap_yc():
        out = []
        for m, other in enumerate((across, mate, corner)):
            spot = tap2.at[2 * y + core]
            out.append(remote(spot, spot, u_send.at[m], u_recv.at[m], other, head))
        return out

    def edges():
        return [remote(edge.at[a], edge_in.at[a, head], e_send.at[a], e_recv.at[a, head],
                       ctx - 1, last) for a in range(2)]

    @pl.when(gives)
    def _():
        for m in edges():
            m.start()

    for a in range(2, 4):
        own(a).start()
        for m in moves[a]:
            m.start()

    for m in tap_z():
        m.wait_recv()
    total = tap1[0]
    for i in range(1, nz):
        total = total + tap1[i]
    tap2[2 * y + core] = total
    for m in tap_yc():
        m.start()

    for a in range(4):
        own(a).wait()
        for m in moves[a]:
            m.wait_recv()

    @pl.when(takes)
    def _():
        for a in range(2):
            for t in range(nh):
                pltpu.make_async_copy(edge_in.at[a, t], edge_in.at[a, t], e_recv.at[a, t]).wait()
                spot = (pl.ds(rows - 16, 16), pl.ds(t * ch, ch))
                out = pairs[2 + a][1]
                out[spot] = (out[spot].astype(F32) + edge_in[a, t].astype(F32)).astype(BF16)

    for m in tap_yc():
        m.wait_recv()
    total = (tap2[0] + tap2[1]) + (tap2[2] + tap2[3])
    kt_out[...] = total[0:3, :]
    vt_out[...] = total[3:6, :]

    for m in mates:
        m.wait_send()
    for m in begun:
        m.wait_send()
    step_y.wait_send()
    for a in range(4):
        for m in moves[a]:
            m.wait_send()
    for m in tap_z():
        m.wait_send()
    for m in tap_yc():
        m.wait_send()

    @pl.when(gives)
    def _():
        for m in edges():
            m.wait_send()


def scatter(nz, nh, part, att, gq, kf, vf, kt, vt):
    length, ch = att.shape
    rows = length // nh
    count = length // 4
    vm = pl.BlockSpec(memory_space=pltpu.VMEM)
    dma = pltpu.SemaphoreType.DMA
    wide = jax.ShapeDtypeStruct((rows, nh * ch), BF16)
    small = jax.ShapeDtypeStruct((3, ch), F32)
    return pl.pallas_call(
        functools.partial(scatter_kernel, nz, nh),
        out_shape=(wide, wide, wide, wide, small, small),
        in_specs=[vm] * 7,
        out_specs=(vm,) * 6,
        scratch_shapes=[
            pltpu.VMEM((nz, 2 * count, 2 * ch), BF16),
            pltpu.VMEM((9, 2, count, 2 * ch), BF16),
            pltpu.VMEM((9, 2, count, 2 * ch), BF16),
            pltpu.VMEM((9, 2, count, 2 * ch), BF16),
            pltpu.VMEM((9, 2, count, 2 * ch), BF16),
            pltpu.VMEM((2, 2, count, 2 * ch), BF16),
            pltpu.VMEM((2, 2, count, 2 * ch), BF16),
            pltpu.VMEM((count, 2 * ch), BF16),
            pltpu.VMEM((count, 2 * ch), BF16),
            pltpu.VMEM((2, length + 16, ch), F32),
            pltpu.VMEM((length, ch), BF16),
            pltpu.VMEM((length, ch), BF16),
            pltpu.VMEM((2, 16, ch), BF16),
            pltpu.VMEM((2, nh, 16, ch), BF16),
            pltpu.VMEM((nz, 8, ch), F32),
            pltpu.VMEM((4, 8, ch), F32),
            dma((4, nh - 1)), dma((4, nh - 1)), dma((4,)),
            dma((2,)), dma((2, nh)),
            dma(()), dma(()),
            dma((9, 2)), dma((9, 2)),
            dma((9, 2)), dma((9, 2)),
            dma((nz,)), dma((nz,)),
            dma((nz - 1,)), dma((nz - 1,)),
            dma((3,)), dma((3,)),
            dma((2, 2)), dma((2, 2)),
        ],
        compiler_params=pltpu.CompilerParams(
            collective_id=1, has_side_effects=True, vmem_limit_bytes=40 << 20),
        name="scatter",
    )(part, att, gq, kf, vf, kt, vt)


def attention_kernel(block, q_ref, cot_ref, kv_ref, att_ref, gq_ref, part_ref,
                     s_ref, e_ref, att_t, gq_t):
    length, ch = q_ref.shape
    half = ch // 2
    keys = kv_ref.shape[0]
    steps = keys // block
    scaling = half ** (-0.5)
    lanes = lax.broadcasted_iota(jnp.int32, (length, ch), 1)

    def split(x):
        x = x.astype(F32)
        zero = jnp.zeros_like(x)
        return jnp.concatenate(
            [jnp.where(lanes < half, x, zero), jnp.where(lanes < half, zero, x)], axis=0).astype(BF16)

    def dot(a, b, ca, cb):
        return lax.dot_general(a, b, (((ca,), (cb,)), ((), ())), preferred_element_type=F32)

    qs = split(q_ref[...].astype(F32) * scaling)
    cots = split(cot_ref[...])

    def at(i):
        return pl.ds(pl.multiple_of(i * block, block), block)

    def scores(i, top):
        s = dot(kv_ref[at(i), 0:ch], qs, 1, 1)
        s_ref[at(i), :] = s
        return jnp.maximum(top, jnp.max(s.reshape(block // 8, 8, 2 * length), axis=0))

    top = lax.fori_loop(0, steps, scores, jnp.full((8, 2 * length), -jnp.inf, F32))
    top = jnp.max(top, axis=0, keepdims=True)

    att_t[...] = jnp.zeros_like(att_t)
    gq_t[...] = jnp.zeros_like(gq_t)

    def raise_(i, total):
        e = jnp.exp(s_ref[at(i), :] - top)
        eb = e.astype(BF16)
        e_ref[at(i), :] = eb
        att_t[...] += dot(kv_ref[at(i), ch:2 * ch], eb, 0, 0)
        return total + jnp.sum(e.reshape(block // 8, 8, 2 * length), axis=0)

    total = lax.fori_loop(0, steps, raise_, jnp.zeros((8, 2 * length), F32))
    inv = 1.0 / jnp.sum(total, axis=0, keepdims=True)

    def join(x):
        return jnp.concatenate([x[0:half, 0:length], x[half:ch, length:2 * length]], axis=0)

    att = jnp.transpose(join(att_t[...] * inv)).astype(BF16)
    att_ref[...] = att
    prod = jnp.transpose(cot_ref[...].astype(F32) * att.astype(F32))
    offset = jnp.concatenate(
        [jnp.sum(prod[0:half], axis=0, keepdims=True),
         jnp.sum(prod[half:ch], axis=0, keepdims=True)], axis=1)

    def back(i, carry):
        w = e_ref[at(i), :].astype(F32) * inv
        dw = dot(kv_ref[at(i), ch:2 * ch], cots, 1, 1)
        ds = (w * (dw - offset)).astype(BF16)
        part_ref[at(i), 0:ch] = dot(ds, qs, 1, 0).astype(BF16)
        part_ref[at(i), ch:2 * ch] = dot(w.astype(BF16), cots, 1, 0).astype(BF16)
        gq_t[...] += dot(kv_ref[at(i), 0:ch], ds, 0, 0)
        return carry

    lax.fori_loop(0, steps, back, 0)
    gq_ref[...] = (jnp.transpose(join(gq_t[...])) * scaling).astype(BF16)


def attention(q, cot, kv):
    length, ch = q.shape
    flat = kv.reshape(-1, 2 * ch)
    keys = flat.shape[0]
    vm = pl.BlockSpec(memory_space=pltpu.VMEM)
    att, gq, part = pl.pallas_call(
        functools.partial(attention_kernel, 512),
        out_shape=(
            jax.ShapeDtypeStruct((length, ch), BF16),
            jax.ShapeDtypeStruct((length, ch), BF16),
            jax.ShapeDtypeStruct((keys, 2 * ch), BF16),
        ),
        in_specs=[vm] * 3,
        out_specs=(vm,) * 3,
        scratch_shapes=[
            pltpu.VMEM((keys, 2 * length), F32),
            pltpu.VMEM((keys, 2 * length), BF16),
            pltpu.VMEM((ch, 2 * length), F32),
            pltpu.VMEM((ch, 2 * length), F32),
        ],
        compiler_params=pltpu.CompilerParams(vmem_limit_bytes=48 << 20),
        name="attention",
    )(q, cot, flat)
    return att, gq, part.reshape(kv.shape)


def local(query_rows, key_rows, value_rows, cotangent, key_taps, value_taps):
    nz = lax.axis_size("ctx") // 4
    nh = lax.axis_size("head")
    q, cot, kf, vf, kv = gather(
        nz, nh, query_rows, key_rows, value_rows, cotangent, key_taps, value_taps)
    att, gq, part = attention(q, cot, kv)
    return scatter(nz, nh, part, att, gq, kf, vf, key_taps, value_taps)


def solution(mesh):
    rows = P(("ctx", "head"), None)
    taps = P(None, "head")
    return jax.shard_map(
        local,
        mesh=mesh,
        in_specs=(rows, rows, rows, rows, taps, taps),
        out_specs=(rows, rows, rows, rows, taps, taps),
        check_vma=False,
    )
```

```python
import functools

import jax
import jax.numpy as jnp
from jax import lax
from jax.experimental import pallas as pl
from jax.experimental.pallas import tpu as pltpu
from jax.sharding import PartitionSpec as P

MESH = pl.DeviceIdType.MESH
F32 = jnp.float32
JUMP = 5
BF16 = jnp.bfloat16


def place(nz):
    ctx = lax.axis_index("ctx")
    head = lax.axis_index("head")
    core = ctx % 2
    z = (ctx // 2) % nz
    y = ctx // (2 * nz)
    return ctx, head, y, z, core


def ctx_of(nz, y, z, core):
    return (y * nz + z) * 2 + core


def remote(src, dst, send, recv, ctx, head):
    return pltpu.make_async_remote_copy(
        src_ref=src, dst_ref=dst, send_sem=send, recv_sem=recv,
        device_id={"ctx": ctx, "head": head}, device_id_type=MESH,
    )


def greet(sem, ctx, head):
    pl.semaphore_signal(sem, inc=1, device_id={"ctx": ctx, "head": head}, device_id_type=MESH)


def col(h, width):
    return pl.ds(pl.multiple_of(h * width, width), width)


def gather_kernel(nz, nh, q_in, k_in, v_in, cot_in, kt, vt,
                  q_out, cot_out, kf, vf, kv,
                  k_loc, v_loc, halo,
                  a_send, a_recv, a_self, h_send, h_recv,
                  y_send, y_recv, r_send, r_recv, l_send, l_recv, c_send, c_recv, j_send, j_recv):
    ctx, head, y, z, core = place(nz)
    nctx = 4 * nz
    rows = q_in.shape[0]
    ch = q_out.shape[1]
    zr, zl = (z + 1) % nz, (z + nz - 1) % nz
    right, left = ctx_of(nz, y, zr, core), ctx_of(nz, y, zl, core)
    across = ctx_of(nz, 1 - y, z, core)
    mate = ctx_of(nz, y, z, 1 - core)
    last = nh - 1
    gives = (head == last) & (ctx < nctx - 1)
    takes = ctx >= 1

    barrier = pltpu.get_barrier_semaphore()
    for p in range(1, nh):
        greet(barrier, ctx, (head + p) % nh)
    for other in (right, left, across, mate):
        greet(barrier, other, head)
    for side in range(2):
        for step in (JUMP, nz - JUMP):
            greet(barrier, ctx_of(nz, side, (z + step) % nz, core), head)

    @pl.when(takes)
    def _():
        greet(barrier, ctx - 1, last)

    @pl.when(gives)
    def _():
        pl.semaphore_wait(barrier, nh - 1 + 8 + nh)

    @pl.when(jnp.logical_not(gives))
    def _():
        pl.semaphore_wait(barrier, nh - 1 + 8)

    pairs = ((k_in, k_loc), (v_in, v_loc), (q_in, q_out), (cot_in, cot_out))

    def halo_copies():
        out = []
        for a in range(2):
            for t in range(nh):
                out.append(remote(
                    pairs[a][0].at[pl.ds(rows - 16, 16), pl.ds(t * ch, ch)], halo.at[a],
                    h_send.at[a, t], h_recv.at[a], ctx + 1, t))
        return out

    def swaps(a):
        out = []
        for p in range(1, nh):
            t = (head + p) % nh
            out.append(remote(
                pairs[a][0].at[:, col(t, ch)], pairs[a][1].at[col(head, rows), :],
                a_send.at[a, p - 1], a_recv.at[a, p - 1], ctx, t))
        return out

    def own(a):
        return pltpu.make_async_copy(
            pairs[a][0].at[:, col(head, ch)], pairs[a][1].at[col(head, rows), :], a_self.at[a])

    moves = [swaps(a) for a in range(4)]
    for a in range(2):
        own(a).start()
        for m in moves[a]:
            m.start()

    @pl.when(gives)
    def _():
        for m in halo_copies():
            m.start()

    @pl.when(jnp.logical_not(takes))
    def _():
        kf[0:8, :] = jnp.zeros((8, ch), F32)
        vf[0:8, :] = jnp.zeros((8, ch), F32)

    @pl.when(takes)
    def _():
        for a, f in ((0, kf), (1, vf)):
            pltpu.make_async_copy(halo.at[a], halo.at[a], h_recv.at[a]).wait()
            f[0:8, :] = halo[a].astype(F32)[8:16, :]

    count = nh * rows // 4
    for a, f, taps in ((0, kf, kt), (1, vf, vt)):
        own(a).wait()
        for m in moves[a]:
            m.wait_recv()
        f[pl.ds(8, nh * rows), :] = pairs[a][1][...].astype(F32)
        packed = (taps[0:1, :] * f[pl.ds(7, count, stride=4), :]
                  + taps[1:2, :] * f[pl.ds(8, count, stride=4), :]
                  + taps[2:3, :] * f[pl.ds(9, count, stride=4), :])
        kv[core, z, pl.ds(pl.multiple_of(y * count, count), count), a * ch:(a + 1) * ch] = packed.astype(BF16)

    def chunk(zz, u):
        side = y + u - 2 * u * y
        return kv.at[core, zz, pl.ds(pl.multiple_of(side * count, count), count), :]

    def to_mate(zz, u, n):
        return remote(chunk(zz, u), chunk(zz, u), c_send.at[n, u], c_recv.at[n, u], mate, head)

    flows = ((0, 2, 2), (-JUMP, nz // 2 - JUMP, nz // 2 - 1 - JUMP), (JUMP, 2, 2))

    def to_right(f, k, u):
        here = chunk((z + flows[f][0] - k + 2 * nz) % nz, u)
        return remote(here, here, r_send.at[3 * f + k, u], r_recv.at[3 * f + k, u], right, head)

    def to_left(f, k, u):
        here = chunk((z + left_of[f] + k + 2 * nz) % nz, u)
        return remote(here, here, l_send.at[3 * f + k, u], l_recv.at[3 * f + k, u], left, head)

    left_of = (0, JUMP, -JUMP)

    def jump(sign, u):
        side = y + u - 2 * u * y
        here = chunk(z, 0)
        return remote(here, here, j_send.at[sign, u], j_recv.at[sign, u],
                      ctx_of(nz, side, (z + (2 * sign - 1) * JUMP + nz) % nz, core), head)

    step_y = remote(chunk(z, 0), chunk(z, 0), y_send, y_recv, across, head)
    mates = []

    def forward(zz, u, n):
        mates.append(to_mate(zz, u, n))
        mates[-1].start()

    begun = []

    def go(copy):
        copy.start()
        begun.append(copy)

    for sign in range(2):
        go(jump(sign, 0))
    go(to_right(0, 0, 0))
    go(to_left(0, 0, 0))
    step_y.start()
    for sign in range(2):
        go(jump(sign, 1))
    forward(z, 0, 0)
    for a in range(2, 4):
        own(a).start()
        for m in moves[a]:
            m.start()

    def got_right(f, k, u):
        to_right(f, k, u).wait_recv()
        if k + 1 < flows[f][1]:
            go(to_right(f, k + 1, u))
        forward((z - 1 + flows[f][0] - k + 2 * nz) % nz, u, 1 + 3 * f + k)

    def got_left(f, k, u):
        to_left(f, k, u).wait_recv()
        if k + 1 < flows[f][2]:
            go(to_left(f, k + 1, u))
        forward((z + 1 + left_of[f] + k + 2 * nz) % nz, u, 10 + 3 * f + k)

    got_right(0, 0, 0)
    got_left(0, 0, 0)
    step_y.wait_recv()
    go(to_right(0, 0, 1))
    go(to_left(0, 0, 1))
    forward(z, 1, 0)
    for u in range(2):
        for sign in (1, 0):
            jump(sign, u).wait_recv()
            if sign == 1:
                go(to_right(1, 0, u))
                go(to_left(2, 0, u))
            else:
                go(to_right(2, 0, u))
                go(to_left(1, 0, u))
            forward((z - (2 * sign - 1) * JUMP + nz) % nz, u, 19 + sign)
    got_right(0, 1, 0)
    got_left(0, 1, 0)
    got_right(0, 0, 1)
    got_left(0, 0, 1)
    for k in range(3):
        for u in range(2):
            for f in (1, 2):
                if k < flows[f][1]:
                    got_right(f, k, u)
                if k < flows[f][2]:
                    got_left(f, k, u)
        if k == 0:
            got_right(0, 1, 1)
            got_left(0, 1, 1)
    for a in range(2, 4):
        own(a).wait()
        for m in moves[a]:
            m.wait_recv()
    for m in mates:
        m.wait()
    for m in begun:
        m.wait_send()
    step_y.wait_send()
    for a in range(4):
        for m in moves[a]:
            m.wait_send()

    @pl.when(gives)
    def _():
        for m in halo_copies():
            m.wait_send()


def gather(nz, nh, q, k, v, cot, kt, vt):
    rows, width = q.shape
    ch = width // nh
    length = nh * rows
    count = length // 4
    vm = pl.BlockSpec(memory_space=pltpu.VMEM)
    dma = pltpu.SemaphoreType.DMA
    return pl.pallas_call(
        functools.partial(gather_kernel, nz, nh),
        out_shape=(
            jax.ShapeDtypeStruct((length, ch), BF16),
            jax.ShapeDtypeStruct((length, ch), BF16),
            jax.ShapeDtypeStruct((length + 8, ch), F32),
            jax.ShapeDtypeStruct((length + 8, ch), F32),
            jax.ShapeDtypeStruct((2, nz, 2 * count, 2 * ch), BF16),
        ),
        in_specs=[pl.BlockSpec(memory_space=pltpu.HBM)] * 4 + [vm] * 2,
        out_specs=(vm,) * 5,
        scratch_shapes=[
            pltpu.VMEM((length, ch), BF16),
            pltpu.VMEM((length, ch), BF16),
            pltpu.VMEM((2, 16, ch), BF16),
            dma((4, nh - 1)), dma((4, nh - 1)), dma((4,)),
            dma((2, nh)), dma((2,)),
            dma(()), dma(()),
            dma((9, 2)), dma((9, 2)),
            dma((9, 2)), dma((9, 2)),
            dma((21, 2)), dma((21, 2)),
            dma((2, 2)), dma((2, 2)),
        ],
        compiler_params=pltpu.CompilerParams(
            collective_id=0, has_side_effects=True, vmem_limit_bytes=40 << 20),
        name="gather",
    )(q, k, v, cot, kt, vt)


def scatter_kernel(nz, nh, part, att_in, gq_in, kf, vf, kt, vt,
                   att_out, gq_out, gk_out, gv_out, kt_out, vt_out,
                   pin, rbuf, rout, lbuf, lout, jbuf, jout, ybuf, yout, spread, gk_loc, gv_loc,
                   edge, edge_in, tap1, tap2,
                   a_send, a_recv, a_self, e_send, e_recv,
                   y_send, y_recv, r_send, r_recv, l_send, l_recv, c_send, c_recv,
                   t_send, t_recv, u_send, u_recv, j_send, j_recv):
    ctx, head, y, z, core = place(nz)
    nctx = 4 * nz
    rows = att_out.shape[0]
    ch = att_in.shape[1]
    count = nh * rows // 4
    zr, zl = (z + 1) % nz, (z + nz - 1) % nz
    right, left = ctx_of(nz, y, zr, core), ctx_of(nz, y, zl, core)
    across = ctx_of(nz, 1 - y, z, core)
    mate = ctx_of(nz, y, z, 1 - core)
    corner = ctx_of(nz, 1 - y, z, 1 - core)
    last = nh - 1
    takes = (head == last) & (ctx < nctx - 1)
    gives = ctx >= 1

    barrier = pltpu.get_barrier_semaphore()
    for p in range(1, nh):
        greet(barrier, ctx, (head + p) % nh)
    for p in range(1, nz):
        greet(barrier, ctx_of(nz, y, (z + p) % nz, core), head)
    for other in (across, mate, corner):
        greet(barrier, other, head)

    @pl.when(takes)
    def _():
        for t in range(nh):
            greet(barrier, ctx + 1, t)

    @pl.when(gives)
    def _():
        pl.semaphore_wait(barrier, nh - 1 + nz - 1 + 3 + 1)

    @pl.when(jnp.logical_not(gives))
    def _():
        pl.semaphore_wait(barrier, nh - 1 + nz - 1 + 3)


    def to_mate(zz, n):
        return remote(part.at[1 - core, zz], pin.at[zz], c_send.at[n], c_recv.at[n], mate, head)

    offsets = (-8, 7, 3, -3, -7, 6, 4, -4, -6, -5, 5, -2, 2, -1, 1, 0)
    order = [(z + o + 2 * nz) % nz for o in offsets]
    mates = [to_mate(zz, n) for n, zz in enumerate(order)]
    for m in mates:
        m.start()

    pairs = ((att_in, att_out), (gq_in, gq_out), (gk_loc, gk_out), (gv_loc, gv_out))

    def swaps(a):
        out = []
        for p in range(1, nh):
            t = (head + p) % nh
            out.append(remote(
                pairs[a][0].at[col(t, rows), :], pairs[a][1].at[:, col(head, ch)],
                a_send.at[a, p - 1], a_recv.at[a, p - 1], ctx, t))
        return out

    def own(a):
        return pltpu.make_async_copy(
            pairs[a][0].at[col(head, rows), :], pairs[a][1].at[:, col(head, ch)], a_self.at[a])

    moves = [swaps(a) for a in range(4)]
    def part_of(u):
        side = 1 - y - u + 2 * u * y
        return pl.ds(pl.multiple_of(side * count, count), count)

    def local_sum(o, u):
        n = offsets.index(o)
        if u == 0:
            mates[n].wait_recv()
        zz = order[n]
        return part[core, zz, part_of(u), :].astype(F32) + pin[zz, part_of(u), :].astype(F32)

    lefts = ((-8, -7, -6), (3, 4), (-2, -1))
    rights = ((7, 6), (-3, -4), (2, 1))

    def to_right(f, k, u):
        return remote(rout.at[3 * f + k, u], rbuf.at[3 * f + k, u],
                      r_send.at[3 * f + k, u], r_recv.at[3 * f + k, u], right, head)

    def to_left(f, k, u):
        return remote(lout.at[3 * f + k, u], lbuf.at[3 * f + k, u],
                      l_send.at[3 * f + k, u], l_recv.at[3 * f + k, u], left, head)

    def jump(sign, u):
        return remote(jout.at[sign, u], jbuf.at[sign, u], j_send.at[sign, u], j_recv.at[sign, u],
                      ctx_of(nz, y, (z + (2 * sign - 1) * JUMP + nz) % nz, core), head)

    begun = []

    def from_left(f, k, u):
        to_right(f, k, u).wait_recv()
        return rbuf[3 * f + k, u].astype(F32)

    def from_right(f, k, u):
        to_left(f, k, u).wait_recv()
        return lbuf[3 * f + k, u].astype(F32)

    def push_right(f, k, u):
        total = local_sum(rights[f][k], u)
        if k > 0:
            total = total + from_left(f, k - 1, u)
        rout[3 * f + k, u] = total.astype(BF16)
        begun.append(to_right(f, k, u))
        begun[-1].start()

    def push_left(f, k, u):
        total = local_sum(lefts[f][k], u)
        if k > 0:
            total = total + from_right(f, k - 1, u)
        lout[3 * f + k, u] = total.astype(BF16)
        begun.append(to_left(f, k, u))
        begun[-1].start()

    def push_jump(sign, total, u):
        jout[sign, u] = total.astype(BF16)
        begun.append(jump(sign, u))
        begun[-1].start()

    for k in range(2):
        for u in range(2):
            push_left(0, k, u)
            push_right(0, k, u)
            push_left(1, k, u)
            push_right(1, k, u)
        if k == 0:
            for a in range(2):
                own(a).start()
                for m in moves[a]:
                    m.start()
    for u in range(2):
        push_left(0, 2, u)
    for u in range(2):
        push_left(2, 0, u)
        push_right(2, 0, u)
    for u in range(2):
        push_jump(1, local_sum(5, u) + from_left(0, 1, u) + from_right(1, 1, u), u)
    for u in range(2):
        push_left(2, 1, u)
        push_right(2, 1, u)
        push_jump(0, local_sum(-5, u) + from_right(0, 2, u) + from_left(1, 1, u), u)
    for u in range(2):
        total = local_sum(0, u) + from_right(2, 1, u) + from_left(2, 1, u)
        for sign in range(2):
            jump(sign, u).wait_recv()
            total = total + jbuf[sign, u].astype(F32)
        if u == 0:
            ybuf[...] = total.astype(BF16)
            step_y = remote(ybuf, yout, y_send, y_recv, across, head)
            step_y.start()
        else:
            step_y.wait_recv()
            grads = total + yout[...].astype(F32)

    tap1[z, 6:8, :] = jnp.zeros((2, ch), F32)
    for a, f in ((0, kf), (1, vf)):
        g = grads[:, a * ch:(a + 1) * ch]
        for t in range(3):
            tap1[z, 3 * a + t:3 * a + t + 1, :] = jnp.sum(
                g * f[pl.ds(7 + t, count, stride=4), :], axis=0, keepdims=True)

    def tap_z():
        out = []
        for p in range(1, nz):
            out.append(remote(tap1.at[z], tap1.at[z], t_send.at[p - 1], t_recv.at[p - 1],
                              ctx_of(nz, y, (z + p) % nz, core), head))
        return out

    for m in tap_z():
        m.start()

    for a, taps, loc in ((0, kt, gk_loc), (1, vt, gv_loc)):
        g = grads[:, a * ch:(a + 1) * ch]
        spread[a, 0:8, :] = jnp.zeros((8, ch), F32)
        spread[a, pl.ds(nh * rows, 8), :] = jnp.zeros((8, ch), F32)
        spread[a, pl.ds(7, count, stride=4), :] = taps[0:1, :] * g
        spread[a, pl.ds(8, count, stride=4), :] = taps[1:2, :] * g
        spread[a, pl.ds(9, count, stride=4), :] = taps[2:3, :] * g
        spread[a, pl.ds(10, count, stride=4), :] = jnp.zeros((count, ch), F32)
        spread[a, pl.ds(nh * rows + 7, 1), :] = jnp.zeros((1, ch), F32)
        loc[...] = spread[a, pl.ds(8, nh * rows), :].astype(BF16)
        edge[a] = jnp.concatenate([jnp.zeros((8, ch), F32), spread[a, 0:8, :]], axis=0).astype(BF16)

    def tap_yc():
        out = []
        for m, other in enumerate((across, mate, corner)):
            spot = tap2.at[2 * y + core]
            out.append(remote(spot, spot, u_send.at[m], u_recv.at[m], other, head))
        return out

    def edges():
        return [remote(edge.at[a], edge_in.at[a, head], e_send.at[a], e_recv.at[a, head],
                       ctx - 1, last) for a in range(2)]

    @pl.when(gives)
    def _():
        for m in edges():
            m.start()

    for a in range(2, 4):
        own(a).start()
        for m in moves[a]:
            m.start()

    for m in tap_z():
        m.wait_recv()
    total = tap1[0]
    for i in range(1, nz):
        total = total + tap1[i]
    tap2[2 * y + core] = total
    for m in tap_yc():
        m.start()

    for a in range(4):
        own(a).wait()
        for m in moves[a]:
            m.wait_recv()

    @pl.when(takes)
    def _():
        for a in range(2):
            for t in range(nh):
                pltpu.make_async_copy(edge_in.at[a, t], edge_in.at[a, t], e_recv.at[a, t]).wait()
                spot = (pl.ds(rows - 16, 16), pl.ds(t * ch, ch))
                out = pairs[2 + a][1]
                out[spot] = (out[spot].astype(F32) + edge_in[a, t].astype(F32)).astype(BF16)

    for m in tap_yc():
        m.wait_recv()
    total = (tap2[0] + tap2[1]) + (tap2[2] + tap2[3])
    kt_out[...] = total[0:3, :]
    vt_out[...] = total[3:6, :]

    for m in mates:
        m.wait_send()
    for m in begun:
        m.wait_send()
    step_y.wait_send()
    for a in range(4):
        for m in moves[a]:
            m.wait_send()
    for m in tap_z():
        m.wait_send()
    for m in tap_yc():
        m.wait_send()

    @pl.when(gives)
    def _():
        for m in edges():
            m.wait_send()


def scatter(nz, nh, part, att, gq, kf, vf, kt, vt):
    length, ch = att.shape
    rows = length // nh
    count = length // 4
    vm = pl.BlockSpec(memory_space=pltpu.VMEM)
    dma = pltpu.SemaphoreType.DMA
    wide = jax.ShapeDtypeStruct((rows, nh * ch), BF16)
    small = jax.ShapeDtypeStruct((3, ch), F32)
    return pl.pallas_call(
        functools.partial(scatter_kernel, nz, nh),
        out_shape=(wide, wide, wide, wide, small, small),
        in_specs=[vm] * 7,
        out_specs=(vm,) * 6,
        scratch_shapes=[
            pltpu.VMEM((nz, 2 * count, 2 * ch), BF16),
            pltpu.VMEM((9, 2, count, 2 * ch), BF16),
            pltpu.VMEM((9, 2, count, 2 * ch), BF16),
            pltpu.VMEM((9, 2, count, 2 * ch), BF16),
            pltpu.VMEM((9, 2, count, 2 * ch), BF16),
            pltpu.VMEM((2, 2, count, 2 * ch), BF16),
            pltpu.VMEM((2, 2, count, 2 * ch), BF16),
            pltpu.VMEM((count, 2 * ch), BF16),
            pltpu.VMEM((count, 2 * ch), BF16),
            pltpu.VMEM((2, length + 16, ch), F32),
            pltpu.VMEM((length, ch), BF16),
            pltpu.VMEM((length, ch), BF16),
            pltpu.VMEM((2, 16, ch), BF16),
            pltpu.VMEM((2, nh, 16, ch), BF16),
            pltpu.VMEM((nz, 8, ch), F32),
            pltpu.VMEM((4, 8, ch), F32),
            dma((4, nh - 1)), dma((4, nh - 1)), dma((4,)),
            dma((2,)), dma((2, nh)),
            dma(()), dma(()),
            dma((9, 2)), dma((9, 2)),
            dma((9, 2)), dma((9, 2)),
            dma((nz,)), dma((nz,)),
            dma((nz - 1,)), dma((nz - 1,)),
            dma((3,)), dma((3,)),
            dma((2, 2)), dma((2, 2)),
        ],
        compiler_params=pltpu.CompilerParams(
            collective_id=1, has_side_effects=True, vmem_limit_bytes=40 << 20),
        name="scatter",
    )(part, att, gq, kf, vf, kt, vt)


def attention_kernel(block, q_ref, cot_ref, kv_ref, att_ref, gq_ref, part_ref,
                     s_ref, e_ref, att_t, gq_t):
    length, ch = q_ref.shape
    half = ch // 2
    keys = kv_ref.shape[0]
    steps = keys // block
    scaling = half ** (-0.5)
    lanes = lax.broadcasted_iota(jnp.int32, (length, ch), 1)

    def split(x):
        x = x.astype(F32)
        zero = jnp.zeros_like(x)
        return jnp.concatenate(
            [jnp.where(lanes < half, x, zero), jnp.where(lanes < half, zero, x)], axis=0).astype(BF16)

    def dot(a, b, ca, cb):
        return lax.dot_general(a, b, (((ca,), (cb,)), ((), ())), preferred_element_type=F32)

    qs = split(q_ref[...].astype(F32) * scaling)
    cots = split(cot_ref[...])

    def at(i):
        return pl.ds(pl.multiple_of(i * block, block), block)

    def scores(i, top):
        s = dot(kv_ref[at(i), 0:ch], qs, 1, 1)
        s_ref[at(i), :] = s
        return jnp.maximum(top, jnp.max(s.reshape(block // 8, 8, 2 * length), axis=0))

    top = lax.fori_loop(0, steps, scores, jnp.full((8, 2 * length), -jnp.inf, F32))
    top = jnp.max(top, axis=0, keepdims=True)

    att_t[...] = jnp.zeros_like(att_t)
    gq_t[...] = jnp.zeros_like(gq_t)

    def raise_(i, total):
        e = jnp.exp(s_ref[at(i), :] - top)
        eb = e.astype(BF16)
        e_ref[at(i), :] = eb
        att_t[...] += dot(kv_ref[at(i), ch:2 * ch], eb, 0, 0)
        return total + jnp.sum(e.reshape(block // 8, 8, 2 * length), axis=0)

    total = lax.fori_loop(0, steps, raise_, jnp.zeros((8, 2 * length), F32))
    inv = 1.0 / jnp.sum(total, axis=0, keepdims=True)

    def join(x):
        return jnp.concatenate([x[0:half, 0:length], x[half:ch, length:2 * length]], axis=0)

    att = jnp.transpose(join(att_t[...] * inv)).astype(BF16)
    att_ref[...] = att
    prod = jnp.transpose(cot_ref[...].astype(F32) * att.astype(F32))
    offset = jnp.concatenate(
        [jnp.sum(prod[0:half], axis=0, keepdims=True),
         jnp.sum(prod[half:ch], axis=0, keepdims=True)], axis=1)

    def back(i, carry):
        w = e_ref[at(i), :].astype(F32) * inv
        dw = dot(kv_ref[at(i), ch:2 * ch], cots, 1, 1)
        ds = (w * (dw - offset)).astype(BF16)
        part_ref[at(i), 0:ch] = dot(ds, qs, 1, 0).astype(BF16)
        part_ref[at(i), ch:2 * ch] = dot(w.astype(BF16), cots, 1, 0).astype(BF16)
        gq_t[...] += dot(kv_ref[at(i), 0:ch], ds, 0, 0)
        return carry

    lax.fori_loop(0, steps, back, 0)
    gq_ref[...] = (jnp.transpose(join(gq_t[...])) * scaling).astype(BF16)


def attention(q, cot, kv):
    length, ch = q.shape
    flat = kv.reshape(-1, 2 * ch)
    keys = flat.shape[0]
    vm = pl.BlockSpec(memory_space=pltpu.VMEM)
    att, gq, part = pl.pallas_call(
        functools.partial(attention_kernel, 512),
        out_shape=(
            jax.ShapeDtypeStruct((length, ch), BF16),
            jax.ShapeDtypeStruct((length, ch), BF16),
            jax.ShapeDtypeStruct((keys, 2 * ch), BF16),
        ),
        in_specs=[vm] * 3,
        out_specs=(vm,) * 3,
        scratch_shapes=[
            pltpu.VMEM((keys, 2 * length), F32),
            pltpu.VMEM((keys, 2 * length), BF16),
            pltpu.VMEM((ch, 2 * length), F32),
            pltpu.VMEM((ch, 2 * length), F32),
        ],
        compiler_params=pltpu.CompilerParams(vmem_limit_bytes=48 << 20),
        name="attention",
    )(q, cot, flat)
    return att, gq, part.reshape(kv.shape)


def local(query_rows, key_rows, value_rows, cotangent, key_taps, value_taps):
    nz = lax.axis_size("ctx") // 4
    nh = lax.axis_size("head")
    q, cot, kf, vf, kv = gather(
        nz, nh, query_rows, key_rows, value_rows, cotangent, key_taps, value_taps)
    att, gq, part = attention(q, cot, kv)
    return scatter(nz, nh, part, att, gq, kf, vf, key_taps, value_taps)


def solution(mesh):
    rows = P(("ctx", "head"), None)
    taps = P(None, "head")
    return jax.shard_map(
        local,
        mesh=mesh,
        in_specs=(rows, rows, rows, rows, taps, taps),
        out_specs=(rows, rows, rows, rows, taps, taps),
        check_vma=False,
    )
```
